128 devices in a mesh: group: 8 (over z, core), sub: 16 (over y, x).
Axes of the slice: x: 4, y: 4, z: 4, core: 2. Of those that a mesh axis runs over, the one named last changes fastest.
Arguments:
- adjoint: float32 [4, 256, 262144], P(None, None, ('group', 'sub')), may hold values from -6 to 6
- velocity: bfloat16 [3, 256, 262144], P(None, None, ('group', 'sub')), may hold values from -6 to 6
- face_speed: bfloat16 [216, 262144], P(None, ('group', 'sub')), may hold values from -6 to 6
- derivatives: bfloat16 [768, 256], replicated, may hold values from -0.375 to 0.375
- lift_operator: bfloat16 [256, 216], replicated, may hold values from -1 to 1
- emission_profile: bfloat16 [256, 32], replicated, may hold values from -0.046875 to 0.046875
- neighbours: int32 [6, 262144], P(None, ('group', 'sub')), may hold values from 0 to 3327, as said below
- sub_sends: int32 [4, 131072], P(None, ('group', 'sub')), may hold values from 0 to 2047, as said below
- group_sends: int32 [2, 32768], P(None, ('group', 'sub')), may hold values from 0 to 2047, as said below
- element_tile: int32 [262144], P(('group', 'sub')), may hold values from 0 to 4095
- tile_slot: int32 [4096], replicated, may hold values from 0 to 4095, as said below
Outputs:
- adjoint_next: float32 [4, 256, 262144], P(None, None, ('group', 'sub'))
- emission_grad: float32 [4096, 128], P(('group', 'sub'))
The draws below stay inside these ranges and needn't reach their ends.
Inputs may be any that keep to these rules, and one draw needn't show every extreme that they name: `neighbours`: faces pair up symmetrically: face 2a + 1 of an element meets face 2a of exactly one element. Positions below 2048 name an element of the same partition; positions 2048 + r * 64 + j name slot j from partition r of the group, and are used only for faces 0 to 3; positions from 3072 on name the adjacent group's slots and are used only for faces 4 and 5. `sub_sends`: column (p * 16 + r) * 64 + j is partition p's slot j for partition r of its group. Between two distinct partitions of a group the same number of face pairs, 16 to 64, crosses in each of faces 0 and 1 and of faces 2 and 3, filling slots 0 onwards; in every group some pair has 64. Unused slots, and a partition's slots for itself, name element 0 and are read by nobody. `group_sends`: column p * 256 + j is partition p's slot j. Partitions of the same index q in adjacent groups share 256 // 2 to 256 face pairs, the same number for every group, filling slots 0 onwards; some q has 256. Unused slots name element 0 and are read by nobody. `tile_slot`: A permutation of the tiles onto the rows.
All inputs are finite; a program needn't handle non-finite values.
Results may differ from the reference program's by a relative error of at most 0.0032.
Values may be sent and summed in bfloat16 or wider, within the bound.
No kernel may reach another device: no remote copies, remote signals or barrier semaphores. Data moves between devices by JAX's collectives and lax.ppermute only.
A program may use at most 192 MiB of HBM per device.

```python
import jax
import jax.numpy as jnp
import numpy as np
from jax import lax

ORDER = 5
NODES = 256
FACE = 36
TRACER_KINDS = 4
EMIT_HEIGHTS = 32
PART_ELEMENTS = 2048
CAP = 64
VCAP = 256
GROUPS = 8
SUBPARTS = 16
ELEMS = 262144
TILES = 4096
GROUP_TILES = 512


def mesh_lists(key):
    device_count = GROUPS * SUBPARTS
    block_len = PART_ELEMENTS // SUBPARTS
    low_count = max(1, CAP // 4)
    vertical_low = max(1, VCAP // 2)
    key_counts, key_first, key_second, key_vertical, key_vpick, key_shuffle = jax.random.split(key, 6)
    counts_raw = jax.random.randint(key_counts, (2, GROUPS, SUBPARTS, SUBPARTS), low_count, CAP + 1)
    row_ids = jnp.arange(SUBPARTS)[:, None]
    col_ids = jnp.arange(SUBPARTS)[None, :]
    pair_counts = jnp.where(row_ids < col_ids, counts_raw, jnp.swapaxes(counts_raw, 2, 3))
    first_pick = jax.random.randint(key_first, (2, GROUPS, 1, 1), 0, SUBPARTS)
    second_pick = (first_pick + jax.random.randint(key_second, (2, GROUPS, 1, 1), 1, SUBPARTS)) % SUBPARTS
    forced = (row_ids == first_pick) & (col_ids == second_pick) | (row_ids == second_pick) & (col_ids == first_pick)
    pair_counts = jnp.where(forced, CAP, pair_counts)
    pair_counts = jnp.where(row_ids == col_ids, 0, pair_counts)
    vertical_counts = jax.random.randint(key_vertical, (SUBPARTS,), vertical_low, VCAP + 1)
    vertical_pick = jax.random.randint(key_vpick, (), 0, SUBPARTS)
    vertical_counts = jnp.where(jnp.arange(SUBPARTS) == vertical_pick, VCAP, vertical_counts)

    def shuffled(subkey):
        return jax.random.permutation(subkey, PART_ELEMENTS).astype(jnp.int32)
    relabels = jax.vmap(shuffled)(jax.random.split(key_shuffle, device_count * 3)).reshape(device_count, 3, PART_ELEMENTS)

    def per_device(group_id, sub_id, relabel_all):
        structural = jnp.arange(PART_ELEMENTS, dtype=jnp.int32)
        offset_in = structural % block_len
        block_ids = structural // block_len
        slot_ids = jnp.arange(CAP, dtype=jnp.int32)
        vertical_slots = jnp.arange(VCAP, dtype=jnp.int32)
        peer_ids = jnp.arange(SUBPARTS, dtype=jnp.int32)[:, None]
        position_rows = []
        send_rows = []
        for axis_id in range(2):
            relabel = relabel_all[axis_id]
            peer_counts = pair_counts[axis_id, group_id, sub_id]
            crossing = peer_counts[block_ids]
            forward_local = relabel[block_ids * block_len + (offset_in + 1) % block_len]
            forward = jnp.where(offset_in < crossing, PART_ELEMENTS + block_ids * CAP + offset_in, forward_local)
            behind_local = relabel[block_ids * block_len + (offset_in - 1) % block_len]
            behind_remote = (offset_in >= 1) & (offset_in <= crossing)
            behind = jnp.where(behind_remote, PART_ELEMENTS + block_ids * CAP + offset_in - 1, behind_local)
            position_rows.append(jnp.zeros(PART_ELEMENTS, jnp.int32).at[relabel].set(behind))
            position_rows.append(jnp.zeros(PART_ELEMENTS, jnp.int32).at[relabel].set(forward))
            valid = slot_ids[None, :] < peer_counts[:, None]
            minus_elem = relabel[peer_ids * block_len + jnp.minimum(slot_ids[None, :] + 1, block_len - 1)]
            plus_elem = relabel[peer_ids * block_len + slot_ids[None, :]]
            send_rows.append(jnp.where(valid, minus_elem, 0).reshape(-1))
            send_rows.append(jnp.where(valid, plus_elem, 0).reshape(-1))
        relabel = relabel_all[2]
        vertical_reach = vertical_counts[sub_id]
        group_base = PART_ELEMENTS + SUBPARTS * CAP
        forward = jnp.where(structural < vertical_reach, group_base + structural, relabel[(structural + 1) % PART_ELEMENTS])
        behind_remote = (structural >= 1) & (structural <= vertical_reach)
        behind = jnp.where(behind_remote, group_base + structural - 1, relabel[(structural - 1) % PART_ELEMENTS])
        position_rows.append(jnp.zeros(PART_ELEMENTS, jnp.int32).at[relabel].set(behind))
        position_rows.append(jnp.zeros(PART_ELEMENTS, jnp.int32).at[relabel].set(forward))
        down_list = jnp.where(vertical_slots < vertical_reach, relabel[jnp.minimum(vertical_slots + 1, PART_ELEMENTS - 1)], 0)
        up_list = jnp.where(vertical_slots < vertical_reach, relabel[vertical_slots], 0)
        return (jnp.stack(position_rows), jnp.stack(send_rows), jnp.stack([down_list, up_list]))
    device_ids = jnp.arange(device_count, dtype=jnp.int32)
    positions, sends, vertical = jax.vmap(per_device)(device_ids // SUBPARTS, device_ids % SUBPARTS, relabels)
    positions = jnp.transpose(positions, (1, 0, 2)).reshape(6, device_count * PART_ELEMENTS)
    sends = jnp.transpose(sends, (1, 0, 2)).reshape(4, device_count * SUBPARTS * CAP)
    vertical = jnp.transpose(vertical, (1, 0, 2)).reshape(2, device_count * VCAP)
    return (positions.astype(jnp.int32), sends.astype(jnp.int32), vertical.astype(jnp.int32))


def draw_neighbours(key, part):
    return mesh_lists(jax.random.fold_in(key, 11))[0]


def draw_sub_sends(key, part):
    return mesh_lists(jax.random.fold_in(key, 11))[1]


def draw_group_sends(key, part):
    return mesh_lists(jax.random.fold_in(key, 11))[2]


def draw_element_tile(key, part):
    return jax.random.randint(key, (ELEMS,), 0, TILES).astype(jnp.int32)


def draw_tile_slot(key, part):

    def shuffled(subkey):
        return jax.random.permutation(subkey, GROUP_TILES).astype(jnp.int32)
    shuffles = jax.vmap(shuffled)(jax.random.split(key, GROUPS))
    bases = jnp.arange(GROUPS, dtype=jnp.int32)[:, None] * GROUP_TILES
    return (shuffles + bases).reshape(-1).astype(jnp.int32)


def levels(stream_key, extent, pieces, low, largest):
    factor_of, own = 1.0, jax.random.fold_in(stream_key, 6)
    for axis_at, blocks in pieces:
        heights = jnp.exp(jax.random.uniform(jax.random.fold_in(own, axis_at), (blocks,), jnp.float32, low / len(pieces), largest / len(pieces)))
        factor_of = factor_of * jnp.repeat(heights, extent[axis_at] // blocks).reshape([-1 if axis == axis_at else 1 for axis in range(len(extent))])
    return factor_of


def bell_draw(own_key, dims, deviation, limit, cuts=(), kind=jnp.bfloat16):
    loudness = levels(own_key, dims, cuts, -0.22, 0.18) if cuts else 1.0
    result = jax.random.normal(own_key, dims, jnp.float32) * deviation * loudness
    return jnp.minimum(jnp.maximum(result, -limit), limit).astype(kind)


def setup_inputs(seed: int = 0) -> dict:
    splits = jax.random.split(jax.random.key(seed), 12)
    adjoint = bell_draw(splits[0], (TRACER_KINDS, NODES, ELEMS), 1.0, 6.0, ((2, 128),), jnp.float32)
    velocity = bell_draw(splits[1], (3, NODES, ELEMS), 1.0, 6.0, ((2, 128),))
    face_speed = bell_draw(splits[2], (6 * FACE, ELEMS), 1.0, 6.0, ((1, 128),))
    derivatives = bell_draw(splits[3], (3 * NODES, NODES), NODES ** -0.5, 0.375)
    lift_operator = bell_draw(splits[4], (NODES, 6 * FACE), FACE ** -0.5, 1.0)
    emission_profile = bell_draw(splits[5], (NODES, EMIT_HEIGHTS), (NODES * PART_ELEMENTS * SUBPARTS // GROUP_TILES) ** -0.5, 0.046875)
    neighbours = draw_neighbours(jax.random.fold_in(splits[11], 71), 0)
    sub_sends = draw_sub_sends(jax.random.fold_in(splits[11], 71), 0)
    group_sends = draw_group_sends(jax.random.fold_in(splits[11], 71), 0)
    element_tile = draw_element_tile(jax.random.fold_in(splits[11], 71), 0)
    tile_slot = draw_tile_slot(jax.random.fold_in(splits[11], 71), 0)
    return {"adjoint": adjoint, "velocity": velocity, "face_speed": face_speed, "derivatives": derivatives, "lift_operator": lift_operator, "emission_profile": emission_profile, "neighbours": neighbours, "sub_sends": sub_sends, "group_sends": group_sends, "element_tile": element_tile, "tile_slot": tile_slot}


SECTION = 0.125


def face_table(order):
    edge_nodes = order + 1
    coords_a, coords_b = np.meshgrid(np.arange(edge_nodes), np.arange(edge_nodes), indexing="ij")
    coords_a = coords_a.reshape(-1)
    coords_b = coords_b.reshape(-1)
    face_rows = []
    for axis_id in range(3):
        for level_id in (0, edge_nodes - 1):
            fixed_col = coords_a * 0 + level_id
            if axis_id == 0:
                triple = (fixed_col, coords_a, coords_b)
            elif axis_id == 1:
                triple = (coords_a, fixed_col, coords_b)
            else:
                triple = (coords_a, coords_b, fixed_col)
            face_rows.append((triple[0] * edge_nodes + triple[1]) * edge_nodes + triple[2])
    return np.stack(face_rows).astype(np.int32)


def reference(adjoint, velocity, face_speed, derivatives, lift_operator, emission_profile, neighbours, sub_sends, group_sends, element_tile, tile_slot):
    face_rows = jnp.asarray(face_table(ORDER))
    device_count = GROUPS * SUBPARTS
    adjoint_lowered = lax.optimization_barrier(adjoint.astype(jnp.bfloat16))

    def columns(array, device_id, length):
        return lax.dynamic_slice_in_dim(array, device_id * length, length, array.ndim - 1)

    def build_sends(device_id):
        traces = columns(adjoint_lowered, device_id, PART_ELEMENTS)[:, face_rows, :]
        sub_list = columns(sub_sends, device_id, SUBPARTS * CAP)
        group_list = columns(group_sends, device_id, VCAP)
        sub_out = jnp.stack([jnp.take(traces[:, face_id], sub_list[face_id], axis=2) for face_id in range(4)])
        group_out = jnp.stack([jnp.take(traces[:, 4], group_list[0], axis=2), jnp.take(traces[:, 5], group_list[1], axis=2)])
        return sub_out, group_out

    sub_bufs, group_bufs = lax.map(build_sends, jnp.arange(device_count, dtype=jnp.int32))
    derivative_broad = derivatives.astype(jnp.float32)
    lift_broad = lift_operator.astype(jnp.float32)
    profile_broad = emission_profile.astype(jnp.float32)
    empty_sub = jnp.zeros((TRACER_KINDS, FACE, SUBPARTS * CAP), jnp.bfloat16)
    empty_group = jnp.zeros((TRACER_KINDS, FACE, VCAP), jnp.bfloat16)

    def one_device(running_total, device_id):
        group_id = device_id // SUBPARTS
        sub_id = device_id % SUBPARTS
        peer_bufs = lax.dynamic_slice_in_dim(sub_bufs, group_id * SUBPARTS, SUBPARTS, 0)
        for_me = lax.dynamic_slice_in_dim(peer_bufs, sub_id * CAP, CAP, 4)
        received = jnp.transpose(for_me, (1, 2, 3, 0, 4)).reshape(4, TRACER_KINDS, FACE, SUBPARTS * CAP)
        below_id = ((group_id + GROUPS - 1) % GROUPS) * SUBPARTS + sub_id
        above_id = ((group_id + 1) % GROUPS) * SUBPARTS + sub_id
        from_below = group_bufs[below_id, 1]
        from_above = group_bufs[above_id, 0]
        local_lowered = columns(adjoint_lowered, device_id, PART_ELEMENTS)
        traces = local_lowered[:, face_rows, :]
        nbr_dev = columns(neighbours, device_id, PART_ELEMENTS)
        outside_list = []
        for face_id in range(6):
            trace_id = face_id ^ 1
            sub_part = received[trace_id] if trace_id < 4 else empty_sub
            if trace_id == 5:
                group_part = from_below
            elif trace_id == 4:
                group_part = from_above
            else:
                group_part = empty_group
            pool_rows = jnp.concatenate([traces[:, trace_id], sub_part, group_part], axis=2)
            outside_list.append(jnp.take(pool_rows, nbr_dev[face_id], axis=2))
        outside = jnp.stack(outside_list, axis=1)
        upwind = jnp.maximum(columns(face_speed, device_id, PART_ELEMENTS).astype(jnp.float32), 0.0).reshape(6, FACE, PART_ELEMENTS)
        face_flux_values = (upwind * (outside.astype(jnp.float32) - traces.astype(jnp.float32))).astype(jnp.bfloat16)
        face_flux_values = lax.optimization_barrier(face_flux_values).reshape(TRACER_KINDS, 6 * FACE, PART_ELEMENTS)
        gradient_terms = jnp.einsum("hv,avr->ahr", derivative_broad, local_lowered.astype(jnp.float32))
        vel_dev = columns(velocity, device_id, PART_ELEMENTS).astype(jnp.float32)
        volume = vel_dev[0] * gradient_terms[:, :NODES] + vel_dev[1] * gradient_terms[:, NODES:2 * NODES] + vel_dev[2] * gradient_terms[:, 2 * NODES:]
        lifted_values = jnp.einsum("dq,wqx->wdx", lift_broad, face_flux_values.astype(jnp.float32))
        adjoint_next = columns(adjoint, device_id, PART_ELEMENTS) + SECTION * (volume + lifted_values)
        next_lowered = lax.optimization_barrier(adjoint_next.astype(jnp.bfloat16)).astype(jnp.float32)
        contribution = jnp.einsum("qvx,vj->xqj", next_lowered, profile_broad).reshape(PART_ELEMENTS, TRACER_KINDS * EMIT_HEIGHTS)
        tile_rows = jnp.take(tile_slot, columns(element_tile, device_id, PART_ELEMENTS))
        running_total = running_total + jax.ops.segment_sum(contribution, tile_rows, num_segments=TILES)
        return running_total, adjoint_next

    zero_total = jnp.zeros((TILES, TRACER_KINDS * EMIT_HEIGHTS), jnp.float32)
    totals, stacked = lax.scan(one_device, zero_total, jnp.arange(device_count, dtype=jnp.int32))
    adjoint_next = jnp.transpose(stacked, (1, 2, 0, 3)).reshape(TRACER_KINDS, NODES, device_count * PART_ELEMENTS)
    return adjoint_next, totals
```

```python
import functools

import jax
import jax.numpy as jnp
import numpy as np
from jax import lax
from jax.experimental import pallas as pl
from jax.experimental.pallas import tpu as pltpu
from jax.sharding import PartitionSpec as P

ORDER = 5
SECTION = 0.125
PAD = 40
F32, BF16, I16, I32 = jnp.float32, jnp.bfloat16, jnp.int16, jnp.int32


def face_table(order):
    edge_nodes = order + 1
    coords_a, coords_b = np.meshgrid(np.arange(edge_nodes), np.arange(edge_nodes), indexing="ij")
    coords_a = coords_a.reshape(-1)
    coords_b = coords_b.reshape(-1)
    face_rows = []
    for axis_id in range(3):
        for level_id in (0, edge_nodes - 1):
            fixed_col = coords_a * 0 + level_id
            if axis_id == 0:
                triple = (fixed_col, coords_a, coords_b)
            elif axis_id == 1:
                triple = (coords_a, fixed_col, coords_b)
            else:
                triple = (coords_a, coords_b, fixed_col)
            face_rows.append((triple[0] * edge_nodes + triple[1]) * edge_nodes + triple[2])
    return np.stack(face_rows).astype(np.int32)


def node_selector(nodes):
    table = face_table(ORDER)
    out = np.zeros((6 * PAD, nodes), np.float32)
    for f in range(6):
        for k in range(table.shape[1]):
            out[f * PAD + k, table[f, k]] = 1.0
    return out


def row_spreader(face_nodes):
    out = np.zeros((6 * PAD, 6 * face_nodes), np.float32)
    for f in range(6):
        for k in range(face_nodes):
            out[f * PAD + k, f * face_nodes + k] = 1.0
    return out


def one_hot(count, positions):
    rows = lax.broadcasted_iota(I16, (count, positions.shape[1]), 0)
    return jnp.where(rows == positions.astype(I16), jnp.ones((), BF16), jnp.zeros((), BF16))


def dot(a, b):
    return jnp.dot(a, b, preferred_element_type=F32)


def send_kernel(adj_ref, sel_ref, ss_ref, gs_ref, pool_ref, send_ref, up_ref, down_ref, *, block):
    step = pl.program_id(0)
    cols = pl.ds(pl.multiple_of(step * block, block), block)
    for pair in range(2):
        first = dot(sel_ref[...], adj_ref[2 * pair].astype(BF16))
        second = dot(sel_ref[...], adj_ref[2 * pair + 1].astype(BF16))
        for f in range(6):
            rows = slice(f * PAD, (f + 1) * PAD)
            both = jnp.concatenate([first[rows], second[rows]], axis=0).astype(BF16)
            pool_ref[f, 2 * PAD * pair : 2 * PAD * (pair + 1), cols] = both

    @pl.when(step == pl.num_programs(0) - 1)
    def _():
        elements = pool_ref.shape[2]
        half = send_ref.shape[3] // 2
        low = lax.broadcasted_iota(I32, (4 * PAD, 2 * half), 1) < half
        for q in range(2):
            a = dot(pool_ref[2 * q], one_hot(elements, ss_ref[2 * q : 2 * q + 1, :]))
            b = dot(pool_ref[2 * q + 1], one_hot(elements, ss_ref[2 * q + 1 : 2 * q + 2, :]))
            for i in range(send_ref.shape[0] // 2):
                lanes = slice(2 * half * i, 2 * half * (i + 1))
                ai, bi = a[:, lanes], b[:, lanes]
                send_ref[2 * i, q] = jnp.where(low, ai, pltpu.roll(bi, half, 1)).astype(BF16)
                send_ref[2 * i + 1, q] = jnp.where(low, pltpu.roll(ai, half, 1), bi).astype(BF16)
        down_ref[...] = dot(pool_ref[4], one_hot(elements, gs_ref[0:1, :])).astype(BF16)
        up_ref[...] = dot(pool_ref[5], one_hot(elements, gs_ref[1:2, :])).astype(BF16)


def local_kernel(nbr_ref, pool_ref, tile_ref, slot_ref, out_ref, row_ref, *, chunk):
    f = pl.program_id(0)
    elements = pool_ref.shape[2]
    positions = nbr_ref[pl.ds(f, 1), :]
    for c in range(0, elements, chunk):
        hot = one_hot(elements, positions[:, c : c + chunk])
        out_ref[0, :, c : c + chunk] = dot(pool_ref[0], hot).astype(BF16)

    @pl.when(f == 0)
    def _():
        tiles = slot_ref.shape[1]
        slot = slot_ref[...]
        sub = lax.broadcasted_iota(I32, (16, tiles), 0)
        high = jnp.broadcast_to(jnp.right_shift(slot, 6), (16, tiles))
        lowd = jnp.broadcast_to(jnp.bitwise_and(slot, 63), (16, tiles))
        digits = jnp.where(sub == 0, high, jnp.where(sub == 1, lowd, 0)).astype(F32).astype(BF16)
        for c in range(0, elements, chunk):
            found = dot(digits, one_hot(tiles, tile_ref[:, c : c + chunk]))
            row_ref[:, c : c + chunk] = (found[0:1] * 64.0 + found[1:2]).astype(I32)


def volume_kernel(adj_ref, vel_ref, der_ref, out_ref):
    nodes = adj_ref.shape[1]
    for s in range(adj_ref.shape[0]):
        adj = adj_ref[s]
        g = dot(der_ref[...], adj.astype(BF16))
        vol = vel_ref[0].astype(F32) * g[:nodes]
        vol += vel_ref[1].astype(F32) * g[nodes : 2 * nodes]
        vol += vel_ref[2].astype(F32) * g[2 * nodes :]
        out_ref[s] = adj + SECTION * vol


def update_kernel(
    nbr_ref, pool_ref, loc_ref, recv_ref, below_ref, above_ref, fs_ref, spread_ref, lift_ref, prof_ref, base_ref,
    next_ref, contrib_ref, rpool, lift_pad, flux, *, elements,
):
    step = pl.program_id(0)
    peers, _, _, width = recv_ref.shape
    half = width // 2
    species = base_ref.shape[0]

    @pl.when(step == 0)
    def _():
        low = lax.broadcasted_iota(I32, (4 * PAD, width), 1) < half
        for q in range(2):
            for i in range(peers // 2):
                lanes = slice(width * i, width * (i + 1))
                x = recv_ref[2 * i, q].astype(F32)
                y = recv_ref[2 * i + 1, q].astype(F32)
                rpool[2 * q, :, lanes] = jnp.where(low, x, pltpu.roll(y, half, 1)).astype(BF16)
                rpool[2 * q + 1, :, lanes] = jnp.where(low, pltpu.roll(x, half, 1), y).astype(BF16)
        lift_pad[...] = lax.dot_general(
            lift_ref[...], spread_ref[...], (((1,), (1,)), ((), ())), preferred_element_type=F32
        ).astype(BF16)

    upwind = dot(spread_ref[...], jnp.maximum(fs_ref[...], jnp.zeros((), BF16)))
    slots = peers * half
    for q in range(3):
        parts = []
        for f in (2 * q, 2 * q + 1):
            t = f ^ 1
            if t < 4:
                hot = one_hot(slots, nbr_ref[f : f + 1, :] - elements)
                far = dot(rpool[t], hot)
            else:
                source = below_ref if t == 5 else above_ref
                hot = one_hot(source.shape[1], nbr_ref[f : f + 1, :] - (elements + slots))
                far = dot(source[...], hot)
            gap = (loc_ref[f].astype(F32) + far) - pool_ref[f].astype(F32)
            up = upwind[f * PAD : (f + 1) * PAD]
            parts.append([up * gap[s * PAD : (s + 1) * PAD] for s in range(species)])
        for s in range(species):
            both = jnp.concatenate([parts[0][s], parts[1][s]], axis=0).astype(BF16)
            flux[s, 2 * PAD * q : 2 * PAD * (q + 1), :] = both
    terms = []
    for s in range(species):
        value = base_ref[s] + SECTION * dot(lift_pad[...], flux[s])
        next_ref[s] = value
        terms.append(
            lax.dot_general(
                prof_ref[...], value.astype(BF16), (((0,), (0,)), ((), ())), preferred_element_type=F32
            )
        )
    contrib = jnp.transpose(jnp.concatenate(terms, axis=0))
    high = contrib.astype(BF16)
    contrib_ref[:, : contrib.shape[1]] = high
    contrib_ref[:, contrib.shape[1] :] = (contrib - high.astype(F32)).astype(BF16)


def scatter_kernel(row_ref, contrib_ref, out_ref):
    block, width = out_ref.shape
    first = pl.program_id(0) * block
    hot = one_hot(block, row_ref[...] - first)
    both = dot(hot, contrib_ref[...])
    out_ref[...] = (both[:, :width] + both[:, width:]).astype(BF16)


def whole(*shape):
    return pl.BlockSpec(shape, lambda i: (0,) * len(shape))


def params():
    return pltpu.CompilerParams(vmem_limit_bytes=48 * 1024 * 1024)


def cost(flops, nbytes):
    return pl.CostEstimate(flops=flops, bytes_accessed=nbytes, transcendentals=0)


def on_device(
    adjoint, velocity, face_speed, derivatives, lift_operator, emission_profile,
    neighbours, sub_sends, group_sends, element_tile, tile_slot,
):
    species, nodes, elements = adjoint.shape
    peers = lax.axis_size("sub")
    groups = lax.axis_size("group")
    slots = sub_sends.shape[1]
    half = slots // peers
    vcap = group_sends.shape[1]
    tiles = tile_slot.shape[0]
    heights = emission_profile.shape[1]
    face_rows = face_speed.shape[0]
    sel = jnp.asarray(node_selector(nodes), BF16)
    spread = jnp.asarray(row_spreader(face_rows // 6), BF16)
    rows = species * PAD
    sds = jax.ShapeDtypeStruct
    block = 512
    steps = elements // block

    pool, send, up, down = pl.pallas_call(
        functools.partial(send_kernel, block=block),
        grid=(steps,),
        in_specs=[
            pl.BlockSpec((species, nodes, block), lambda i: (0, 0, i)),
            whole(6 * PAD, nodes), whole(4, slots), whole(2, vcap),
        ],
        out_specs=[whole(6, rows, elements), whole(peers, 2, rows, 2 * half), whole(rows, vcap), whole(rows, vcap)],
        out_shape=[
            sds((6, rows, elements), BF16), sds((peers, 2, rows, 2 * half), BF16),
            sds((rows, vcap), BF16), sds((rows, vcap), BF16),
        ],
        compiler_params=params(),
        cost_estimate=cost(12_000_000_000, 14_000_000),
        name="sends",
    )(adjoint, sel, sub_sends, group_sends)

    received = lax.all_to_all(send, "sub", split_axis=0, concat_axis=0, tiled=True)
    ring_up = [(g, (g + 1) % groups) for g in range(groups)]
    ring_down = [(g, (g - 1) % groups) for g in range(groups)]
    from_below = lax.ppermute(up, "group", ring_up)
    from_above = lax.ppermute(down, "group", ring_down)

    local, tile_rows = pl.pallas_call(
        functools.partial(local_kernel, chunk=1024),
        grid=(6,),
        in_specs=[
            whole(6, elements),
            pl.BlockSpec((1, rows, elements), lambda f: (f + 1 - 2 * (f % 2), 0, 0)),
            whole(1, elements), whole(1, tiles),
        ],
        out_specs=[pl.BlockSpec((1, rows, elements), lambda f: (f, 0, 0)), whole(1, elements)],
        out_shape=[sds((6, rows, elements), BF16), sds((1, elements), I32)],
        compiler_params=params(),
        cost_estimate=cost(12_000_000_000, 8_000_000),
        name="local",
    )(neighbours, pool, element_tile.reshape(1, elements), tile_slot.reshape(1, tiles))

    base = pl.pallas_call(
        volume_kernel,
        grid=(steps,),
        in_specs=[
            pl.BlockSpec((species, nodes, block), lambda i: (0, 0, i)),
            pl.BlockSpec((3, nodes, block), lambda i: (0, 0, i)),
            whole(3 * nodes, nodes),
        ],
        out_specs=pl.BlockSpec((species, nodes, block), lambda i: (0, 0, i)),
        out_shape=sds((species, nodes, elements), F32),
        compiler_params=params(),
        cost_estimate=cost(3_200_000_000, 20_000_000),
        name="volume",
    )(adjoint, velocity, derivatives)

    adjoint_next, contrib = pl.pallas_call(
        functools.partial(update_kernel, elements=elements),
        grid=(steps,),
        in_specs=[
            pl.BlockSpec((6, block), lambda i: (0, i)),
            pl.BlockSpec((6, rows, block), lambda i: (0, 0, i)),
            pl.BlockSpec((6, rows, block), lambda i: (0, 0, i)),
            whole(peers, 2, rows, 2 * half), whole(rows, vcap), whole(rows, vcap),
            pl.BlockSpec((face_rows, block), lambda i: (0, i)),
            whole(6 * PAD, face_rows), whole(nodes, face_rows), whole(nodes, heights),
            pl.BlockSpec((species, nodes, block), lambda i: (0, 0, i)),
        ],
        out_specs=[
            pl.BlockSpec((species, nodes, block), lambda i: (0, 0, i)),
            pl.BlockSpec((block, 2 * species * heights), lambda i: (i, 0)),
        ],
        out_shape=[sds((species, nodes, elements), F32), sds((elements, 2 * species * heights), BF16)],
        scratch_shapes=[
            pltpu.VMEM((4, rows, slots), BF16), pltpu.VMEM((nodes, 6 * PAD), BF16),
            pltpu.VMEM((species, 6 * PAD, block), BF16),
        ],
        compiler_params=params(),
        cost_estimate=cost(8_000_000_000, 28_000_000),
        name="update",
    )(
        neighbours, pool, local, received, from_below, from_above, face_speed, spread,
        lift_operator, emission_profile, base,
    )

    width = species * heights
    row_block = 512
    partial = pl.pallas_call(
        scatter_kernel,
        grid=(tiles // row_block,),
        in_specs=[whole(1, elements), whole(elements, 2 * width)],
        out_specs=pl.BlockSpec((row_block, width), lambda i: (i, 0)),
        out_shape=sds((tiles, width), BF16),
        compiler_params=params(),
        cost_estimate=cost(4_300_000_000, 2_000_000),
        name="scatter",
    )(tile_rows, contrib)

    devices = groups * peers
    pieces = lax.all_to_all(
        partial.reshape(devices, tiles // devices, width), ("group", "sub"), split_axis=0, concat_axis=0
    )
    emission_grad = jnp.sum(pieces.astype(F32), axis=0)
    return adjoint_next, emission_grad


def solution(mesh):
    both = ("group", "sub")
    placed = (
        P(None, None, both), P(None, None, both), P(None, both), P(), P(), P(),
        P(None, both), P(None, both), P(None, both), P(both), P(),
    )
    return jax.shard_map(
        on_device,
        mesh=mesh,
        in_specs=placed,
        out_specs=(P(None, None, both), P(both, None)),
        check_vma=False,
    )
```

```python
import functools

import jax
import jax.numpy as jnp
import numpy as np
from jax import lax
from jax.experimental import pallas as pl
from jax.experimental.pallas import tpu as pltpu
from jax.sharding import Mesh, PartitionSpec as P

ORDER = 5
SECTION = 0.125
MIB = 1024 * 1024
PAD = 40
F32, BF16, I16, I32 = jnp.float32, jnp.bfloat16, jnp.int16, jnp.int32


def face_table(order):
    edge_nodes = order + 1
    coords_a, coords_b = np.meshgrid(np.arange(edge_nodes), np.arange(edge_nodes), indexing="ij")
    coords_a = coords_a.reshape(-1)
    coords_b = coords_b.reshape(-1)
    face_rows = []
    for axis_id in range(3):
        for level_id in (0, edge_nodes - 1):
            fixed_col = coords_a * 0 + level_id
            if axis_id == 0:
                triple = (fixed_col, coords_a, coords_b)
            elif axis_id == 1:
                triple = (coords_a, fixed_col, coords_b)
            else:
                triple = (coords_a, coords_b, fixed_col)
            face_rows.append((triple[0] * edge_nodes + triple[1]) * edge_nodes + triple[2])
    return np.stack(face_rows).astype(np.int32)


def node_selector(nodes):
    table = face_table(ORDER)
    out = np.zeros((6 * PAD, nodes), np.float32)
    for f in range(6):
        for k in range(table.shape[1]):
            out[f * PAD + k, table[f, k]] = 1.0
    return out


def row_spreader(face_nodes):
    out = np.zeros((6 * PAD, 6 * face_nodes), np.float32)
    for f in range(6):
        for k in range(face_nodes):
            out[f * PAD + k, f * face_nodes + k] = 1.0
    return out


def one_hot(count, positions):
    rows = lax.broadcasted_iota(I16, (count, positions.shape[1]), 0)
    return jnp.where(rows == positions.astype(I16), jnp.ones((), BF16), jnp.zeros((), BF16))


def dot(a, b):
    return jnp.dot(a, b, preferred_element_type=F32)


def send_kernel(adj_ref, sel_ref, ss_ref, gs_ref, pool_ref, send_ref, up_ref, down_ref, *, block):
    step = pl.program_id(0)
    cols = pl.ds(pl.multiple_of(step * block, block), block)
    for pair in range(2):
        picked = [dot(sel_ref[...], adj_ref[s].astype(BF16)) for s in (2 * pair, 2 * pair + 1)]
        for f in range(6):
            rows = slice(f * PAD, (f + 1) * PAD)
            both = jnp.concatenate([picked[0][rows], picked[1][rows]], axis=0).astype(BF16)
            pool_ref[f, 2 * PAD * pair : 2 * PAD * (pair + 1), cols] = both

    @pl.when(step == pl.num_programs(0) - 1)
    def _():
        elements = pool_ref.shape[2]
        half = send_ref.shape[3] // 2
        low = lax.broadcasted_iota(I32, (4 * PAD, 2 * half), 1) < half
        for q in range(2):
            a = dot(pool_ref[2 * q], one_hot(elements, ss_ref[2 * q : 2 * q + 1, :]))
            b = dot(pool_ref[2 * q + 1], one_hot(elements, ss_ref[2 * q + 1 : 2 * q + 2, :]))
            for i in range(send_ref.shape[0] // 2):
                lanes = slice(2 * half * i, 2 * half * (i + 1))
                ai, bi = a[:, lanes], b[:, lanes]
                send_ref[2 * i, q] = jnp.where(low, ai, pltpu.roll(bi, half, 1)).astype(BF16)
                send_ref[2 * i + 1, q] = jnp.where(low, pltpu.roll(ai, half, 1), bi).astype(BF16)
        down_ref[...] = dot(pool_ref[4], one_hot(elements, gs_ref[0:1, :])).astype(BF16)
        up_ref[...] = dot(pool_ref[5], one_hot(elements, gs_ref[1:2, :])).astype(BF16)


def local_kernel(
    adj_ref, vel_ref, der_ref, nbr_ref, pool_hbm, tile_ref, slot_ref, base_ref, gap_ref, row_ref, pool, mixed, sems,
):
    step = pl.program_id(0)
    species, nodes, block = adj_ref.shape
    group = 16
    copies = [pltpu.make_async_copy(pool_hbm.at[f], pool.at[f], sems.at[f]) for f in range(6)]

    @pl.when(step == 0)
    def _():
        for copy in copies:
            copy.start()
        for d in range(3):
            for b in range(nodes // group):
                rows = der_ref[d * nodes + b * group : d * nodes + (b + 1) * group, :]
                mixed[(3 * b + d) * group : (3 * b + d + 1) * group, :] = rows * jnp.asarray(SECTION, BF16)

    for s in range(species):
        g = dot(mixed[...], adj_ref[s].astype(BF16))
        for b in range(nodes // group):
            rows = slice(b * group, (b + 1) * group)
            total = adj_ref[s, rows]
            for d in range(3):
                total += vel_ref[d, rows].astype(F32) * g[(3 * b + d) * group : (3 * b + d + 1) * group]
            base_ref[s, rows] = total

    @pl.when(step == 0)
    def _():
        high = slot_ref.shape[0]
        elements = tile_ref.shape[1]
        slot = jnp.transpose(slot_ref[...].astype(F32))
        upper = jnp.floor(slot * (1.0 / 64.0))
        digits = jnp.concatenate([upper, slot - 64.0 * upper], axis=0).astype(BF16)
        lanes = slot_ref.shape[1]
        for c in range(0, elements, block):
            tile = tile_ref[:, c : c + block]
            shift = lanes.bit_length() - 1
            found = dot(digits, one_hot(high, jnp.right_shift(tile, shift)))
            rows = 64.0 * found[:lanes] + found[lanes:]
            within = lax.broadcasted_iota(I32, rows.shape, 0) == jnp.bitwise_and(tile, lanes - 1)
            row_ref[:, c : c + block] = jnp.sum(jnp.where(within, rows, 0.0), axis=0, keepdims=True).astype(I32)
        for copy in copies:
            copy.wait()

    cols = pl.ds(pl.multiple_of(step * block, block), block)
    for f in range(6):
        hot = one_hot(pool.shape[2], nbr_ref[f : f + 1, :])
        gap_ref[f] = dot(pool[f ^ 1], hot) - pool[f, :, cols].astype(F32)


def update_kernel(
    nbr_ref, gap_ref, recv_ref, below_ref, above_ref, fs_ref, spread_ref, lift_ref, prof_ref, base_ref,
    next_ref, contrib_ref, rpool, lift_pad, flux, *, elements,
):
    step = pl.program_id(0)
    peers, _, _, width = recv_ref.shape
    half = width // 2
    species = base_ref.shape[0]

    @pl.when(step == 0)
    def _():
        low = lax.broadcasted_iota(I32, (4 * PAD, width), 1) < half
        for q in range(2):
            for i in range(peers // 2):
                lanes = slice(width * i, width * (i + 1))
                x = recv_ref[2 * i, q].astype(F32)
                y = recv_ref[2 * i + 1, q].astype(F32)
                rpool[2 * q, :, lanes] = jnp.where(low, x, pltpu.roll(y, half, 1)).astype(BF16)
                rpool[2 * q + 1, :, lanes] = jnp.where(low, pltpu.roll(x, half, 1), y).astype(BF16)
        lift_pad[...] = (SECTION * jnp.transpose(dot(spread_ref[...], lift_ref[...]))).astype(BF16)

    upwind = dot(spread_ref[...], jnp.maximum(fs_ref[...], jnp.zeros((), BF16)))
    slots = peers * half
    for q in range(3):
        parts = []
        for f in (2 * q, 2 * q + 1):
            t = f ^ 1
            if t < 4:
                hot = one_hot(slots, nbr_ref[f : f + 1, :] - elements)
                far = dot(rpool[t], hot)
            else:
                source = below_ref if t == 5 else above_ref
                hot = one_hot(source.shape[1], nbr_ref[f : f + 1, :] - (elements + slots))
                far = dot(source[...], hot)
            gap = gap_ref[f] + far
            up = upwind[f * PAD : (f + 1) * PAD]
            parts.append([up * gap[s * PAD : (s + 1) * PAD] for s in range(species)])
        for s in range(species):
            both = jnp.concatenate([parts[0][s], parts[1][s]], axis=0).astype(BF16)
            flux[s, 2 * PAD * q : 2 * PAD * (q + 1), :] = both
    terms = []
    for s in range(species):
        value = base_ref[s] + dot(lift_pad[...], flux[s])
        next_ref[s] = value
        terms.append(dot(prof_ref[...], value.astype(BF16)))
    contrib = jnp.transpose(jnp.concatenate(terms, axis=0))
    high = contrib.astype(BF16)
    contrib_ref[:, : contrib.shape[1]] = high
    contrib_ref[:, contrib.shape[1] :] = (contrib - high.astype(F32)).astype(BF16)


def scatter_kernel(row_ref, contrib_ref, out_ref, *, other):
    block, width = out_ref.shape
    core = lax.axis_index("core")
    half = 1 - core if other else core
    first = (2 * pl.program_id(0) + half) * block
    hot = one_hot(block, row_ref[...] - first)
    both = dot(hot, contrib_ref[...])
    out_ref[...] = both[:, :width] + both[:, width:]


def whole(*shape):
    return pl.BlockSpec(shape, lambda i: (0,) * len(shape))


def params(mib):
    return pltpu.CompilerParams(vmem_limit_bytes=mib * MIB)


def cost(flops, nbytes):
    return pl.CostEstimate(flops=flops, bytes_accessed=nbytes, transcendentals=0)


def on_device(
    adjoint, velocity, face_speed, derivatives, lift_operator, emission_profile,
    neighbours, sub_sends, group_sends, element_tile, tile_slot,
):
    species, nodes, elements = adjoint.shape
    peers = lax.axis_size("sub")
    groups = lax.axis_size("z") * lax.axis_size("core")
    slots = sub_sends.shape[1]
    half = slots // peers
    vcap = group_sends.shape[1]
    tiles = tile_slot.shape[0]
    heights = emission_profile.shape[1]
    face_rows = face_speed.shape[0]
    sel = jnp.asarray(node_selector(nodes), BF16)
    spread = jnp.asarray(row_spreader(face_rows // 6), BF16)
    rows = species * PAD
    sds = jax.ShapeDtypeStruct
    block = 512
    steps = elements // block

    pool, send, up, down = pl.pallas_call(
        functools.partial(send_kernel, block=block),
        grid=(steps,),
        in_specs=[
            pl.BlockSpec((species, nodes, block), lambda i: (0, 0, i)),
            whole(6 * PAD, nodes), whole(4, slots), whole(2, vcap),
        ],
        out_specs=[whole(6, rows, elements), whole(peers, 2, rows, 2 * half), whole(rows, vcap), whole(rows, vcap)],
        out_shape=[
            sds((6, rows, elements), BF16), sds((peers, 2, rows, 2 * half), BF16),
            sds((rows, vcap), BF16), sds((rows, vcap), BF16),
        ],
        compiler_params=params(60),
        cost_estimate=cost(12_000_000_000, 14_000_000),
        name="sends",
    )(adjoint, sel, sub_sends, group_sends)

    received = lax.all_to_all(send, "sub", split_axis=0, concat_axis=0, tiled=True)
    ring_up = [(g, (g + 1) % groups) for g in range(groups)]
    ring_down = [(g, (g - 1) % groups) for g in range(groups)]
    from_below = lax.ppermute(up, ("z", "core"), ring_up)
    from_above = lax.ppermute(down, ("z", "core"), ring_down)

    base, gap, tile_rows = pl.pallas_call(
        local_kernel,
        grid=(steps,),
        in_specs=[
            pl.BlockSpec((species, nodes, block), lambda i: (0, 0, i)),
            pl.BlockSpec((3, nodes, block), lambda i: (0, 0, i)),
            whole(3 * nodes, nodes),
            pl.BlockSpec((6, block), lambda i: (0, i)),
            pl.BlockSpec(memory_space=pl.ANY),
            whole(1, elements), whole(tiles // 128, 128),
        ],
        out_specs=[
            pl.BlockSpec((species, nodes, block), lambda i: (0, 0, i)),
            pl.BlockSpec((6, rows, block), lambda i: (0, 0, i)),
            whole(1, elements),
        ],
        out_shape=[
            sds((species, nodes, elements), F32), sds((6, rows, elements), F32), sds((1, elements), I32),
        ],
        scratch_shapes=[
            pltpu.VMEM((6, rows, elements), BF16), pltpu.VMEM((3 * nodes, nodes), BF16), pltpu.SemaphoreType.DMA((6,)),
        ],
        compiler_params=params(60),
        cost_estimate=cost(16_000_000_000, 32_000_000),
        name="local",
    )(
        adjoint, velocity, derivatives, neighbours, pool, element_tile.reshape(1, elements),
        tile_slot.reshape(tiles // 128, 128),
    )

    adjoint_next, contrib = pl.pallas_call(
        functools.partial(update_kernel, elements=elements),
        grid=(steps,),
        in_specs=[
            pl.BlockSpec((6, block), lambda i: (0, i)),
            pl.BlockSpec((6, rows, block), lambda i: (0, 0, i)),
            whole(peers, 2, rows, 2 * half), whole(rows, vcap), whole(rows, vcap),
            pl.BlockSpec((face_rows, block), lambda i: (0, i)),
            whole(6 * PAD, face_rows), whole(face_rows, nodes), whole(heights, nodes),
            pl.BlockSpec((species, nodes, block), lambda i: (0, 0, i)),
        ],
        out_specs=[
            pl.BlockSpec((species, nodes, block), lambda i: (0, 0, i)),
            pl.BlockSpec((block, 2 * species * heights), lambda i: (i, 0)),
        ],
        out_shape=[sds((species, nodes, elements), F32), sds((elements, 2 * species * heights), BF16)],
        scratch_shapes=[
            pltpu.VMEM((4, rows, slots), BF16), pltpu.VMEM((nodes, 6 * PAD), BF16),
            pltpu.VMEM((species, 6 * PAD, block), BF16),
        ],
        compiler_params=params(56),
        cost_estimate=cost(8_000_000_000, 28_000_000),
        name="update",
    )(
        neighbours, gap, received, from_below, from_above, face_speed, spread,
        lift_operator.T, emission_profile.T, base,
    )

    width = species * heights
    row_block = tiles // groups

    def scattered(other):
        return pl.pallas_call(
            functools.partial(scatter_kernel, other=other),
            grid=(groups // 2,),
            in_specs=[whole(1, elements), whole(elements, 2 * width)],
            out_specs=pl.BlockSpec((row_block, width), lambda i: (i, 0)),
            out_shape=sds((tiles // 2, width), F32),
            compiler_params=params(16),
            cost_estimate=cost(2_100_000_000, 2_000_000),
            name="scatter_other" if other else "scatter_own",
        )(tile_rows, contrib)

    theirs = lax.ppermute(scattered(True), "core", [(0, 1), (1, 0)])
    partial = (scattered(False) + theirs).astype(BF16)
    chips = groups * peers // 2
    pieces = lax.all_to_all(
        partial.reshape(chips, tiles // 2 // chips, width), ("z", "sub"), split_axis=0, concat_axis=0
    )
    emission_grad = jnp.sum(pieces.astype(F32), axis=0)
    return adjoint_next, emission_grad


def solution(mesh):
    groups, peers = mesh.devices.shape
    mesh = Mesh(mesh.devices.reshape(groups // 2, 2, peers), ("z", "core", "sub"))
    both = ("z", "core", "sub")
    placed = (
        P(None, None, both), P(None, None, both), P(None, both), P(), P(), P(),
        P(None, both), P(None, both), P(None, both), P(both), P(),
    )
    return jax.shard_map(
        on_device,
        mesh=mesh,
        in_specs=placed,
        out_specs=(P(None, None, both), P(both, None)),
        check_vma=False,
    )
```

```python
import functools

import jax
import jax.numpy as jnp
import numpy as np
from jax import lax
from jax.experimental import pallas as pl
from jax.experimental.pallas import tpu as pltpu
from jax.sharding import Mesh, PartitionSpec as P

ORDER = 5
SECTION = 0.125
MIB = 1024 * 1024
UPDATE_MIB = 56
MAIN = 32
REST = 4
F32, BF16, I16, I32 = jnp.float32, jnp.bfloat16, jnp.int16, jnp.int32


def face_table(order):
    edge_nodes = order + 1
    coords_a, coords_b = np.meshgrid(np.arange(edge_nodes), np.arange(edge_nodes), indexing="ij")
    coords_a = coords_a.reshape(-1)
    coords_b = coords_b.reshape(-1)
    face_rows = []
    for axis_id in range(3):
        for level_id in (0, edge_nodes - 1):
            fixed_col = coords_a * 0 + level_id
            if axis_id == 0:
                triple = (fixed_col, coords_a, coords_b)
            elif axis_id == 1:
                triple = (coords_a, fixed_col, coords_b)
            else:
                triple = (coords_a, coords_b, fixed_col)
            face_rows.append((triple[0] * edge_nodes + triple[1]) * edge_nodes + triple[2])
    return np.stack(face_rows).astype(np.int32)


def picker(columns, lines):
    out = np.zeros((len(lines), columns), np.float32)
    for row, column in enumerate(lines):
        if column is not None:
            out[row, column] = 1.0
    return jnp.asarray(out, BF16)


def main_picker(faces, first, last):
    table = face_table(ORDER)
    return picker(last - first, [table[f, k] - first for f in faces for k in range(MAIN)])


def rest_picker(species, faces, first, last):
    table = face_table(ORDER)
    return jnp.stack([
        picker(last - first, [
            table[f, MAIN + j] - first if t == s else None
            for f in faces for t in range(species) for j in range(REST)
        ])
        for s in range(species)
    ])


def speed_picker(species, face_nodes):
    lines = [f * face_nodes + k for f in range(6) for k in range(MAIN)]
    lines += [f * face_nodes + MAIN + j for f in range(6) for _ in range(species) for j in range(REST)]
    return picker(6 * face_nodes, lines)


def lift_picker(face_nodes):
    lines = [f * face_nodes + k for f in range(6) for k in range(MAIN)]
    lines += [f * face_nodes + MAIN + j for f in range(6) for j in range(REST)]
    return picker(6 * face_nodes, lines)


def one_hot(count, positions):
    rows = lax.broadcasted_iota(I16, (count, positions.shape[1]), 0)
    return jnp.where(rows == positions.astype(I16), jnp.ones((), BF16), jnp.zeros((), BF16))


def dot(a, b):
    return jnp.dot(a, b, preferred_element_type=F32)


LOW, MID, HIGH = (0, 40), (40, 176), (176, 216)


def send_kernel(
    adj_hbm, main_ref, rest_ref, far_main_ref, far_rest_ref, ss_ref, gs_ref,
    pool_ref, send_ref, up_ref, down_ref, adj, sems,
):
    species = adj.shape[0]
    rows, elements = pool_ref.shape[1:]
    half = send_ref.shape[3] // 2
    copies = [
        pltpu.make_async_copy(adj_hbm.at[:, a:b, :], adj.at[:, a:b, :], sems.at[i])
        for i, (a, b) in enumerate((LOW, HIGH, MID))
    ]
    for copy in copies:
        copy.start()
    low = lax.broadcasted_iota(I32, (rows, 2 * half), 1) < half

    def exchange(q):
        a = dot(pool_ref[2 * q], one_hot(elements, ss_ref[2 * q : 2 * q + 1, :]))
        b = dot(pool_ref[2 * q + 1], one_hot(elements, ss_ref[2 * q + 1 : 2 * q + 2, :]))
        for i in range(send_ref.shape[0] // 2):
            lanes = slice(2 * half * i, 2 * half * (i + 1))
            ai, bi = a[:, lanes], b[:, lanes]
            send_ref[2 * i, q] = jnp.where(low, ai, pltpu.roll(bi, half, 1)).astype(BF16)
            send_ref[2 * i + 1, q] = jnp.where(low, pltpu.roll(ai, half, 1), bi).astype(BF16)

    copies[0].wait()
    copies[1].wait()
    chunk = 1024
    for f, (first, last) in enumerate((LOW, HIGH)):
        for c in range(0, elements, chunk):
            parts = [adj[s, first:last, c : c + chunk].astype(BF16) for s in range(species)]
            rest = sum(dot(rest_ref[f, s], parts[s]) for s in range(species))
            mains = [dot(main_ref[f], parts[s]) for s in range(species)]
            pool_ref[f, :, c : c + chunk] = jnp.concatenate(mains + [rest], axis=0).astype(BF16)
    exchange(0)
    copies[2].wait()
    chunk = 512
    for c in range(0, elements, chunk):
        parts = [adj[s, :, c : c + chunk].astype(BF16) for s in range(species)]
        rest = sum(dot(far_rest_ref[s], parts[s]) for s in range(species))
        mains = [dot(far_main_ref[...], parts[s]) for s in range(species)]
        for i in range(4):
            pieces = [m[MAIN * i : MAIN * (i + 1)] for m in mains]
            pieces.append(rest[species * REST * i : species * REST * (i + 1)])
            pool_ref[2 + i, :, c : c + chunk] = jnp.concatenate(pieces, axis=0).astype(BF16)
    exchange(1)
    down_ref[...] = dot(pool_ref[4], one_hot(elements, gs_ref[0:1, :])).astype(BF16)
    up_ref[...] = dot(pool_ref[5], one_hot(elements, gs_ref[1:2, :])).astype(BF16)


def local_kernel(
    adj_ref, vel_ref, der_ref, nbr_ref, pool_hbm, tile_ref, slot_ref, base_ref, gap_ref, row_ref, pool, mixed, sems,
):
    step = pl.program_id(0)
    species, nodes, block = adj_ref.shape
    group = 16
    copies = [pltpu.make_async_copy(pool_hbm.at[f], pool.at[f], sems.at[f]) for f in range(6)]

    @pl.when(step == 0)
    def _():
        for copy in copies:
            copy.start()
        for d in range(3):
            for b in range(nodes // group):
                rows = der_ref[d * nodes + b * group : d * nodes + (b + 1) * group, :]
                mixed[(3 * b + d) * group : (3 * b + d + 1) * group, :] = rows * jnp.asarray(SECTION, BF16)

    for s in range(species):
        g = dot(mixed[...], adj_ref[s].astype(BF16))
        for b in range(nodes // group):
            rows = slice(b * group, (b + 1) * group)
            total = adj_ref[s, rows]
            for d in range(3):
                total += vel_ref[d, rows].astype(F32) * g[(3 * b + d) * group : (3 * b + d + 1) * group]
            base_ref[s, rows] = total

    @pl.when(step == 0)
    def _():
        high = slot_ref.shape[0]
        elements = tile_ref.shape[1]
        slot = jnp.transpose(slot_ref[...].astype(F32))
        upper = jnp.floor(slot * (1.0 / 64.0))
        digits = jnp.concatenate([upper, slot - 64.0 * upper], axis=0).astype(BF16)
        lanes = slot_ref.shape[1]
        for c in range(0, elements, block):
            tile = tile_ref[:, c : c + block]
            shift = lanes.bit_length() - 1
            found = dot(digits, one_hot(high, jnp.right_shift(tile, shift)))
            rows = 64.0 * found[:lanes] + found[lanes:]
            within = lax.broadcasted_iota(I32, rows.shape, 0) == jnp.bitwise_and(tile, lanes - 1)
            row_ref[:, c : c + block] = jnp.sum(jnp.where(within, rows, 0.0), axis=0, keepdims=True).astype(I32)
        for copy in copies:
            copy.wait()

    cols = pl.ds(pl.multiple_of(step * block, block), block)
    for f in range(6):
        hot = one_hot(pool.shape[2], nbr_ref[f : f + 1, :])
        gap_ref[f] = dot(pool[f ^ 1], hot) - pool[f, :, cols].astype(F32)


def update_kernel(
    nbr_ref, gap_ref, recv_ref, below_ref, above_ref, fs_ref, speed_ref, order_ref, lift_ref, prof_ref, base_ref,
    next_ref, contrib_ref, rpool, lift_sorted, flux, low_next, *, elements,
):
    step = pl.program_id(0)
    peers, _, rows, width = recv_ref.shape
    half = width // 2
    species, nodes, block = base_ref.shape

    def contribute(index):
        terms = [dot(prof_ref[...], low_next[s]) for s in range(species)]
        contrib = jnp.transpose(jnp.concatenate(terms, axis=0))
        high = contrib.astype(BF16)
        lines = pl.ds(pl.multiple_of(index * block, block), block)
        contrib_ref[lines, : contrib.shape[1]] = high
        contrib_ref[lines, contrib.shape[1] :] = (contrib - high.astype(F32)).astype(BF16)

    @pl.when(step == 0)
    def _():
        low = lax.broadcasted_iota(I32, (rows, width), 1) < half
        for q in range(2):
            for i in range(peers // 2):
                lanes = slice(width * i, width * (i + 1))
                x = recv_ref[2 * i, q].astype(F32)
                y = recv_ref[2 * i + 1, q].astype(F32)
                rpool[2 * q, :, lanes] = jnp.where(low, x, pltpu.roll(y, half, 1)).astype(BF16)
                rpool[2 * q + 1, :, lanes] = jnp.where(low, pltpu.roll(x, half, 1), y).astype(BF16)
        lift_sorted[...] = (SECTION * jnp.transpose(dot(order_ref[...], lift_ref[...]))).astype(BF16)
        low_next[...] = jnp.zeros_like(low_next)

    contribute(jnp.maximum(step - 1, 0))
    upwind = dot(speed_ref[...], jnp.maximum(fs_ref[...], jnp.zeros((), BF16)))
    slots = peers * half
    first = lax.broadcasted_iota(I32, (2 * REST, block), 0) < REST
    tails = [[] for _ in range(species)]
    for q in range(3):
        mains, rests = [], []
        for f in (2 * q, 2 * q + 1):
            t = f ^ 1
            if t < 4:
                far = dot(rpool[t], one_hot(slots, nbr_ref[f : f + 1, :] - elements))
            else:
                source = below_ref if t == 5 else above_ref
                hot = one_hot(source.shape[1], nbr_ref[f : f + 1, :] - (elements + slots))
                far = dot(source[...], hot)
            gap = gap_ref[f] + far
            speed = upwind[MAIN * f : MAIN * (f + 1)]
            mains.append([speed * gap[MAIN * s : MAIN * (s + 1)] for s in range(species)])
            line = 6 * MAIN + species * REST * f
            rests.append(upwind[line : line + species * REST] * gap[species * MAIN :])
        for s in range(species):
            both = jnp.concatenate([mains[0][s], mains[1][s]], axis=0).astype(BF16)
            flux[s, 2 * MAIN * q : 2 * MAIN * (q + 1), :] = both
        for v in range(species // 2):
            a = rests[0][2 * REST * v : 2 * REST * (v + 1)]
            b = rests[1][2 * REST * v : 2 * REST * (v + 1)]
            tails[2 * v].append(jnp.where(first, a, pltpu.roll(b, REST, 0)))
            tails[2 * v + 1].append(jnp.where(first, pltpu.roll(a, REST, 0), b))
    for s in range(species):
        flux[s, 6 * MAIN :, :] = jnp.concatenate(tails[s], axis=0).astype(BF16)
    for s in range(species):
        value = base_ref[s] + dot(lift_sorted[...], flux[s])
        next_ref[s] = value
        low_next[s] = value.astype(BF16)

    @pl.when(step == pl.num_programs(0) - 1)
    def _():
        contribute(step)


def scatter_kernel(row_ref, contrib_ref, out_ref, *, other):
    block, width = out_ref.shape
    core = lax.axis_index("core")
    half = 1 - core if other else core
    first = (2 * pl.program_id(0) + half) * block
    hot = one_hot(block, row_ref[...] - first)
    both = dot(hot, contrib_ref[...])
    out_ref[...] = both[:, :width] + both[:, width:]


def whole(*shape):
    return pl.BlockSpec(shape, lambda i: (0,) * len(shape))


def params(mib):
    return pltpu.CompilerParams(vmem_limit_bytes=mib * MIB)


def cost(flops, nbytes):
    return pl.CostEstimate(flops=flops, bytes_accessed=nbytes, transcendentals=0)


def on_device(
    adjoint, velocity, face_speed, derivatives, lift_operator, emission_profile,
    neighbours, sub_sends, group_sends, element_tile, tile_slot,
):
    species, nodes, elements = adjoint.shape
    peers = lax.axis_size("sub")
    groups = lax.axis_size("z") * lax.axis_size("core")
    slots = sub_sends.shape[1]
    half = slots // peers
    vcap = group_sends.shape[1]
    tiles = tile_slot.shape[0]
    heights = emission_profile.shape[1]
    face_rows = face_speed.shape[0]
    rows = species * (MAIN + REST)
    sds = jax.ShapeDtypeStruct
    block = 512
    steps = elements // block

    near = [((f,),) + span for f, span in enumerate((LOW, HIGH))]
    near_main = jnp.stack([main_picker(*where) for where in near])
    near_rest = jnp.stack([rest_picker(species, *where) for where in near])
    far_faces = ((2, 3, 4, 5), 0, HIGH[1])
    vmem = pl.BlockSpec(memory_space=pltpu.VMEM)
    pool, send, up, down = pl.pallas_call(
        send_kernel,
        in_specs=[pl.BlockSpec(memory_space=pl.ANY)] + [vmem] * 6,
        out_specs=[vmem] * 4,
        out_shape=[
            sds((6, rows, elements), BF16), sds((peers, 2, rows, 2 * half), BF16),
            sds((rows, vcap), BF16), sds((rows, vcap), BF16),
        ],
        scratch_shapes=[pltpu.VMEM((species, HIGH[1], elements), F32), pltpu.SemaphoreType.DMA((3,))],
        compiler_params=params(60),
        cost_estimate=cost(12_000_000_000, 14_000_000),
        name="sends",
    )(
        adjoint, near_main, near_rest, main_picker(*far_faces), rest_picker(species, *far_faces),
        sub_sends, group_sends,
    )

    received = lax.all_to_all(send, "sub", split_axis=0, concat_axis=0, tiled=True)
    ring_up = [(g, (g + 1) % groups) for g in range(groups)]
    ring_down = [(g, (g - 1) % groups) for g in range(groups)]
    from_below = lax.ppermute(up, ("z", "core"), ring_up)
    from_above = lax.ppermute(down, ("z", "core"), ring_down)

    base, gap, tile_rows = pl.pallas_call(
        local_kernel,
        grid=(steps,),
        in_specs=[
            pl.BlockSpec((species, nodes, block), lambda i: (0, 0, i)),
            pl.BlockSpec((3, nodes, block), lambda i: (0, 0, i)),
            whole(3 * nodes, nodes),
            pl.BlockSpec((6, block), lambda i: (0, i)),
            pl.BlockSpec(memory_space=pl.ANY),
            whole(1, elements), whole(tiles // 128, 128),
        ],
        out_specs=[
            pl.BlockSpec((species, nodes, block), lambda i: (0, 0, i)),
            pl.BlockSpec((6, rows, block), lambda i: (0, 0, i)),
            whole(1, elements),
        ],
        out_shape=[
            sds((species, nodes, elements), F32), sds((6, rows, elements), F32), sds((1, elements), I32),
        ],
        scratch_shapes=[
            pltpu.VMEM((6, rows, elements), BF16), pltpu.VMEM((3 * nodes, nodes), BF16), pltpu.SemaphoreType.DMA((6,)),
        ],
        compiler_params=params(60),
        cost_estimate=cost(16_000_000_000, 32_000_000),
        name="local",
    )(
        adjoint, velocity, derivatives, neighbours, pool, element_tile.reshape(1, elements),
        tile_slot.reshape(tiles // 128, 128),
    )

    face_nodes = face_rows // 6
    adjoint_next, contrib = pl.pallas_call(
        functools.partial(update_kernel, elements=elements),
        grid=(steps,),
        in_specs=[
            pl.BlockSpec((6, block), lambda i: (0, i)),
            pl.BlockSpec((6, rows, block), lambda i: (0, 0, i)),
            whole(peers, 2, rows, 2 * half), whole(rows, vcap), whole(rows, vcap),
            pl.BlockSpec((face_rows, block), lambda i: (0, i)),
            whole(2 * rows, face_rows), whole(face_rows, face_rows), whole(face_rows, nodes), whole(heights, nodes),
            pl.BlockSpec((species, nodes, block), lambda i: (0, 0, i)),
        ],
        out_specs=[
            pl.BlockSpec((species, nodes, block), lambda i: (0, 0, i)),
            whole(elements, 2 * species * heights),
        ],
        out_shape=[sds((species, nodes, elements), F32), sds((elements, 2 * species * heights), BF16)],
        scratch_shapes=[
            pltpu.VMEM((4, rows, slots), BF16), pltpu.VMEM((nodes, face_rows), BF16),
            pltpu.VMEM((species, face_rows, block), BF16), pltpu.VMEM((species, nodes, block), BF16),
        ],
        compiler_params=params(UPDATE_MIB),
        cost_estimate=cost(8_000_000_000, 28_000_000),
        name="update",
    )(
        neighbours, gap, received, from_below, from_above, face_speed, speed_picker(species, face_nodes),
        lift_picker(face_nodes), lift_operator.T, emission_profile.T, base,
    )

    width = species * heights
    row_block = tiles // groups

    def scattered(other):
        return pl.pallas_call(
            functools.partial(scatter_kernel, other=other),
            grid=(groups // 2,),
            in_specs=[whole(1, elements), whole(elements, 2 * width)],
            out_specs=pl.BlockSpec((row_block, width), lambda i: (i, 0)),
            out_shape=sds((tiles // 2, width), F32),
            compiler_params=params(16),
            cost_estimate=cost(2_100_000_000, 2_000_000),
            name="scatter_other" if other else "scatter_own",
        )(tile_rows, contrib)

    theirs = lax.ppermute(scattered(True), "core", [(0, 1), (1, 0)])
    partial = (scattered(False) + theirs).astype(BF16)
    chips = groups * peers // 2
    pieces = lax.all_to_all(
        partial.reshape(chips, tiles // 2 // chips, width), ("z", "sub"), split_axis=0, concat_axis=0
    )
    emission_grad = jnp.sum(pieces.astype(F32), axis=0)
    return adjoint_next, emission_grad


def solution(mesh):
    groups, peers = mesh.devices.shape
    mesh = Mesh(mesh.devices.reshape(groups // 2, 2, peers), ("z", "core", "sub"))
    both = ("z", "core", "sub")
    placed = (
        P(None, None, both), P(None, None, both), P(None, both), P(), P(), P(),
        P(None, both), P(None, both), P(None, both), P(both), P(),
    )
    return jax.shard_map(
        on_device,
        mesh=mesh,
        in_specs=placed,
        out_specs=(P(None, None, both), P(both, None)),
        check_vma=False,
    )
```

```python
import functools

import jax
import jax.numpy as jnp
import numpy as np
from jax import lax
from jax.experimental import pallas as pl
from jax.experimental.pallas import tpu as pltpu
from jax.sharding import Mesh, PartitionSpec as P

ORDER = 5
SECTION = 0.125
MIB = 1024 * 1024
UPDATE_MIB = 46
MAIN = 32
REST = 4
GROUP_ROWS = 512
F32, BF16, I16, I32 = jnp.float32, jnp.bfloat16, jnp.int16, jnp.int32


def face_table(order):
    edge_nodes = order + 1
    coords_a, coords_b = np.meshgrid(np.arange(edge_nodes), np.arange(edge_nodes), indexing="ij")
    coords_a = coords_a.reshape(-1)
    coords_b = coords_b.reshape(-1)
    face_rows = []
    for axis_id in range(3):
        for level_id in (0, edge_nodes - 1):
            fixed_col = coords_a * 0 + level_id
            if axis_id == 0:
                triple = (fixed_col, coords_a, coords_b)
            elif axis_id == 1:
                triple = (coords_a, fixed_col, coords_b)
            else:
                triple = (coords_a, coords_b, fixed_col)
            face_rows.append((triple[0] * edge_nodes + triple[1]) * edge_nodes + triple[2])
    return np.stack(face_rows).astype(np.int32)


def picker(columns, lines):
    out = np.zeros((len(lines), columns), np.float32)
    for row, column in enumerate(lines):
        if column is not None:
            out[row, column] = 1.0
    return jnp.asarray(out, BF16)


def trace_picker(species, faces, first, last):
    table = face_table(ORDER)
    return jnp.stack([
        picker(last - first, [table[f, k] - first for f in faces for k in range(MAIN)] + [
            table[f, MAIN + j] - first if t == s else None
            for f in faces for t in range(species) for j in range(REST)
        ])
        for s in range(species)
    ])


def speed_picker(species, face_nodes):
    lines = [f * face_nodes + k for f in range(6) for k in range(MAIN)]
    lines += [f * face_nodes + MAIN + j for f in range(6) for _ in range(species) for j in range(REST)]
    return picker(6 * face_nodes, lines)


def lift_picker(face_nodes):
    lines = [f * face_nodes + k for f in range(6) for k in range(MAIN)]
    lines += [f * face_nodes + MAIN + j for f in range(6) for j in range(REST)]
    return picker(6 * face_nodes, lines)


def one_hot(count, positions):
    rows = lax.broadcasted_iota(I16, (count, positions.shape[1]), 0)
    return jnp.where(rows == positions.astype(I16), jnp.ones((), BF16), jnp.zeros((), BF16))


def dot(a, b):
    return jnp.dot(a, b, preferred_element_type=F32)


LOW, MID, HIGH = (0, 40), (40, 176), (176, 216)


def send_kernel(
    adj_hbm, near_ref, far_ref, ss_ref, gs_ref,
    pool_ref, send_ref, up_ref, down_ref, adj, sems,
):
    species = adj.shape[0]
    rows, elements = pool_ref.shape[1:]
    half = send_ref.shape[3] // 2
    copies = [
        pltpu.make_async_copy(adj_hbm.at[:, a:b, :], adj.at[:, a:b, :], sems.at[i])
        for i, (a, b) in enumerate((LOW, HIGH, MID))
    ]
    for copy in copies:
        copy.start()
    low = lax.broadcasted_iota(I32, (rows, 2 * half), 1) < half

    def exchange(q):
        a = dot(pool_ref[2 * q], one_hot(elements, ss_ref[2 * q : 2 * q + 1, :]))
        b = dot(pool_ref[2 * q + 1], one_hot(elements, ss_ref[2 * q + 1 : 2 * q + 2, :]))
        for i in range(send_ref.shape[0] // 2):
            lanes = slice(2 * half * i, 2 * half * (i + 1))
            ai, bi = a[:, lanes], b[:, lanes]
            send_ref[2 * i, q] = jnp.where(low, ai, pltpu.roll(bi, half, 1)).astype(BF16)
            send_ref[2 * i + 1, q] = jnp.where(low, pltpu.roll(ai, half, 1), bi).astype(BF16)

    def fill(faces, picks, first, last, chunk):
        count = len(faces)
        shared = species * REST
        for c in range(0, elements, chunk):
            found = [dot(picks[s], adj[s, first:last, c : c + chunk].astype(BF16)) for s in range(species)]
            rest = sum(x[MAIN * count :] for x in found)
            for i, f in enumerate(faces):
                pieces = [x[MAIN * i : MAIN * (i + 1)] for x in found] + [rest[shared * i : shared * (i + 1)]]
                pool_ref[f, :, c : c + chunk] = jnp.concatenate(pieces, axis=0).astype(BF16)

    copies[0].wait()
    copies[1].wait()
    fill((0,), near_ref[0], *LOW, 1024)
    fill((1,), near_ref[1], *HIGH, 1024)
    exchange(0)
    copies[2].wait()
    fill((2, 3, 4, 5), far_ref[...], 0, HIGH[1], 512)
    exchange(1)
    down_ref[...] = dot(pool_ref[4], one_hot(elements, gs_ref[0:1, :])).astype(BF16)
    up_ref[...] = dot(pool_ref[5], one_hot(elements, gs_ref[1:2, :])).astype(BF16)


def local_kernel(
    adj_ref, vel_ref, der_ref, nbr_ref, pool_hbm, tile_ref, slot_ref, base_ref, gap_ref, row_ref, pool, mixed, sems,
):
    step = pl.program_id(0)
    species, nodes, block = adj_ref.shape
    group = 16
    copies = [pltpu.make_async_copy(pool_hbm.at[f], pool.at[f], sems.at[f]) for f in range(6)]

    @pl.when(step == 0)
    def _():
        for copy in copies:
            copy.start()
        for d in range(3):
            for b in range(nodes // group):
                rows = der_ref[d * nodes + b * group : d * nodes + (b + 1) * group, :]
                mixed[(3 * b + d) * group : (3 * b + d + 1) * group, :] = rows * jnp.asarray(SECTION, BF16)

    for s in range(species):
        g = dot(mixed[...], adj_ref[s].astype(BF16))
        for b in range(nodes // group):
            rows = slice(b * group, (b + 1) * group)
            total = adj_ref[s, rows]
            for d in range(3):
                total += vel_ref[d, rows].astype(F32) * g[(3 * b + d) * group : (3 * b + d + 1) * group]
            base_ref[s, rows] = total

    @pl.when(step == 0)
    def _():
        elements = tile_ref.shape[1]
        high, lanes = slot_ref.shape
        fine = lanes // 2
        slot = jnp.transpose(slot_ref[...].astype(F32))
        upper = jnp.floor(slot * (1.0 / 64.0))
        digits = jnp.concatenate([
            jnp.concatenate([x[:fine], x[fine:]], axis=1) for x in (upper, slot - 64.0 * upper)
        ], axis=0).astype(BF16)
        bits = fine.bit_length() - 1
        for c in range(0, elements, block):
            tile = tile_ref[:, c : c + block]
            coarse = jnp.right_shift(tile, bits)
            place = jnp.bitwise_and(coarse, 1) * high + jnp.right_shift(coarse, 1)
            found = dot(digits, one_hot(2 * high, place))
            rows = 64.0 * found[:fine] + found[fine:]
            within = lax.broadcasted_iota(I32, rows.shape, 0) == jnp.bitwise_and(tile, fine - 1)
            row_ref[:, c : c + block] = jnp.sum(jnp.where(within, rows, 0.0), axis=0, keepdims=True).astype(I32)
        for copy in copies:
            copy.wait()

    cols = pl.ds(pl.multiple_of(step * block, block), block)
    for f in range(6):
        hot = one_hot(pool.shape[2], nbr_ref[f : f + 1, :])
        gap_ref[f] = dot(pool[f ^ 1], hot) - pool[f, :, cols].astype(F32)


def update_kernel(
    nbr_ref, gap_hbm, recv_ref, below_ref, above_ref, fs_ref, speed_ref, order_ref, lift_ref, prof_ref, base_hbm, row_ref,
    next_ref, contrib_ref, other_ref, rpool, lift_sorted, flux, low_next, gap_all, base_all, sems, *, elements,
):
    step = pl.program_id(0)
    peers, _, rows, width = recv_ref.shape
    half = width // 2
    species, nodes, block = next_ref.shape
    steps = gap_all.shape[0]

    def loads(index):
        cols = pl.ds(pl.multiple_of(index * block, block), block)
        return (
            pltpu.make_async_copy(gap_hbm.at[:, :, cols], gap_all.at[index], sems.at[0, index]),
            pltpu.make_async_copy(base_hbm.at[:, :, cols], base_all.at[index], sems.at[1, index]),
        )

    def contribute(index):
        terms = [dot(prof_ref[...], low_next[s]) for s in range(species)]
        contrib = jnp.transpose(jnp.concatenate(terms, axis=0))
        high = contrib.astype(BF16)
        lines = pl.ds(pl.multiple_of(index * block, block), block)
        contrib_ref[lines, : contrib.shape[1]] = high
        contrib_ref[lines, contrib.shape[1] :] = (contrib - high.astype(F32)).astype(BF16)

    @pl.when(step == 0)
    def _():
        for index in range(steps):
            for copy in loads(index):
                copy.start()
        low = lax.broadcasted_iota(I32, (rows, width), 1) < half
        for q in range(2):
            for i in range(peers // 2):
                lanes = slice(width * i, width * (i + 1))
                x = recv_ref[2 * i, q].astype(F32)
                y = recv_ref[2 * i + 1, q].astype(F32)
                rpool[2 * q, :, lanes] = jnp.where(low, x, pltpu.roll(y, half, 1)).astype(BF16)
                rpool[2 * q + 1, :, lanes] = jnp.where(low, pltpu.roll(x, half, 1), y).astype(BF16)
        lift_sorted[...] = (SECTION * jnp.transpose(dot(order_ref[...], lift_ref[...]))).astype(BF16)
        low_next[...] = jnp.zeros_like(low_next)

    for copy in loads(step):
        copy.wait()
    gap_ref, base_ref = gap_all.at[step], base_all.at[step]
    contribute(jnp.maximum(step - 1, 0))
    upwind = dot(speed_ref[...], jnp.maximum(fs_ref[...], jnp.zeros((), BF16)))
    slots = peers * half
    first = lax.broadcasted_iota(I32, (2 * REST, block), 0) < REST
    tails = [[] for _ in range(species)]
    for q in range(3):
        mains, rests = [], []
        for f in (2 * q, 2 * q + 1):
            t = f ^ 1
            if t < 4:
                far = dot(rpool[t], one_hot(slots, nbr_ref[f : f + 1, :] - elements))
            else:
                source = below_ref if t == 5 else above_ref
                hot = one_hot(source.shape[1], nbr_ref[f : f + 1, :] - (elements + slots))
                far = dot(source[...], hot)
            gap = gap_ref[f] + far
            speed = upwind[MAIN * f : MAIN * (f + 1)]
            mains.append([speed * gap[MAIN * s : MAIN * (s + 1)] for s in range(species)])
            line = 6 * MAIN + species * REST * f
            rests.append(upwind[line : line + species * REST] * gap[species * MAIN :])
        for s in range(species):
            both = jnp.concatenate([mains[0][s], mains[1][s]], axis=0).astype(BF16)
            flux[s, 2 * MAIN * q : 2 * MAIN * (q + 1), :] = both
        for v in range(species // 2):
            a = rests[0][2 * REST * v : 2 * REST * (v + 1)]
            b = rests[1][2 * REST * v : 2 * REST * (v + 1)]
            tails[2 * v].append(jnp.where(first, a, pltpu.roll(b, REST, 0)))
            tails[2 * v + 1].append(jnp.where(first, pltpu.roll(a, REST, 0), b))
    for s in range(species):
        flux[s, 6 * MAIN :, :] = jnp.concatenate(tails[s], axis=0).astype(BF16)
    for s in range(species):
        value = base_ref[s] + dot(lift_sorted[...], flux[s])
        next_ref[s] = value
        low_next[s] = value.astype(BF16)

    @pl.when(step == steps - 1)
    def _():
        contribute(step)
        scatter(row_ref, contrib_ref, other_ref, True)


def scatter(row_ref, contrib_ref, out_ref, other):
    width = out_ref.shape[1]
    core = lax.axis_index("core")
    side = 1 - core if other else core
    for i in range(out_ref.shape[0] // GROUP_ROWS):
        hot = one_hot(GROUP_ROWS, row_ref[...] - (2 * i + side) * GROUP_ROWS)
        both = dot(hot, contrib_ref[...])
        out_ref[i * GROUP_ROWS : (i + 1) * GROUP_ROWS, :] = both[:, :width] + both[:, width:]


def own_kernel(row_ref, contrib_ref, out_ref):
    scatter(row_ref, contrib_ref, out_ref, False)


def whole(*shape):
    return pl.BlockSpec(shape, lambda i: (0,) * len(shape))


def params(mib):
    return pltpu.CompilerParams(vmem_limit_bytes=mib * MIB)


def cost(flops, nbytes):
    return pl.CostEstimate(flops=flops, bytes_accessed=nbytes, transcendentals=0)


def on_device(
    adjoint, velocity, face_speed, derivatives, lift_operator, emission_profile,
    neighbours, sub_sends, group_sends, element_tile, tile_slot,
):
    species, nodes, elements = adjoint.shape
    peers = lax.axis_size("sub")
    groups = lax.axis_size("z") * lax.axis_size("core")
    slots = sub_sends.shape[1]
    half = slots // peers
    vcap = group_sends.shape[1]
    tiles = tile_slot.shape[0]
    heights = emission_profile.shape[1]
    face_rows = face_speed.shape[0]
    rows = species * (MAIN + REST)
    sds = jax.ShapeDtypeStruct
    block = 512
    steps = elements // block

    near = jnp.stack([trace_picker(species, (f,), *span) for f, span in enumerate((LOW, HIGH))])
    far = trace_picker(species, (2, 3, 4, 5), 0, HIGH[1])
    vmem = pl.BlockSpec(memory_space=pltpu.VMEM)
    pool, send, up, down = pl.pallas_call(
        send_kernel,
        in_specs=[pl.BlockSpec(memory_space=pl.ANY)] + [vmem] * 4,
        out_specs=[vmem] * 4,
        out_shape=[
            sds((6, rows, elements), BF16), sds((peers, 2, rows, 2 * half), BF16),
            sds((rows, vcap), BF16), sds((rows, vcap), BF16),
        ],
        scratch_shapes=[pltpu.VMEM((species, HIGH[1], elements), F32), pltpu.SemaphoreType.DMA((3,))],
        compiler_params=params(60),
        cost_estimate=cost(12_000_000_000, 14_000_000),
        name="sends",
    )(
        adjoint, near, far, sub_sends, group_sends,
    )

    received = lax.all_to_all(send, "sub", split_axis=0, concat_axis=0, tiled=True)
    ring_up = [(g, (g + 1) % groups) for g in range(groups)]
    ring_down = [(g, (g - 1) % groups) for g in range(groups)]
    from_below = lax.ppermute(up, ("z", "core"), ring_up)
    from_above = lax.ppermute(down, ("z", "core"), ring_down)

    base, gap, tile_rows = pl.pallas_call(
        local_kernel,
        grid=(steps,),
        in_specs=[
            pl.BlockSpec((species, nodes, block), lambda i: (0, 0, i)),
            pl.BlockSpec((3, nodes, block), lambda i: (0, 0, i)),
            whole(3 * nodes, nodes),
            pl.BlockSpec((6, block), lambda i: (0, i)),
            pl.BlockSpec(memory_space=pl.ANY),
            whole(1, elements), whole(tiles // 128, 128),
        ],
        out_specs=[
            pl.BlockSpec((species, nodes, block), lambda i: (0, 0, i)),
            pl.BlockSpec((6, rows, block), lambda i: (0, 0, i)),
            whole(1, elements),
        ],
        out_shape=[
            sds((species, nodes, elements), F32), sds((6, rows, elements), F32), sds((1, elements), I32),
        ],
        scratch_shapes=[
            pltpu.VMEM((6, rows, elements), BF16), pltpu.VMEM((3 * nodes, nodes), BF16), pltpu.SemaphoreType.DMA((6,)),
        ],
        compiler_params=params(60),
        cost_estimate=cost(16_000_000_000, 32_000_000),
        name="local",
    )(
        adjoint, velocity, derivatives, neighbours, pool, element_tile.reshape(1, elements),
        tile_slot.reshape(tiles // 128, 128),
    )

    face_nodes = face_rows // 6
    width = species * heights
    hbm = pl.BlockSpec(memory_space=pltpu.HBM)
    adjoint_next, contrib, for_other = pl.pallas_call(
        functools.partial(update_kernel, elements=elements),
        grid=(steps,),
        in_specs=[
            pl.BlockSpec((6, block), lambda i: (0, i)),
            hbm, whole(peers, 2, rows, 2 * half), whole(rows, vcap), whole(rows, vcap),
            pl.BlockSpec((face_rows, block), lambda i: (0, i)),
            whole(2 * rows, face_rows), whole(face_rows, face_rows), whole(face_rows, nodes), whole(heights, nodes),
            hbm, whole(1, elements),
        ],
        out_specs=[
            pl.BlockSpec((species, nodes, block), lambda i: (0, 0, i)),
            whole(elements, 2 * width), whole(tiles // 2, width),
        ],
        out_shape=[
            sds((species, nodes, elements), F32), sds((elements, 2 * width), BF16), sds((tiles // 2, width), F32),
        ],
        scratch_shapes=[
            pltpu.VMEM((4, rows, slots), BF16), pltpu.VMEM((nodes, face_rows), BF16),
            pltpu.VMEM((species, face_rows, block), BF16), pltpu.VMEM((species, nodes, block), BF16),
            pltpu.VMEM((steps, 6, rows, block), F32), pltpu.VMEM((steps, species, nodes, block), F32),
            pltpu.SemaphoreType.DMA((2, steps)),
        ],
        compiler_params=params(UPDATE_MIB),
        cost_estimate=cost(8_000_000_000, 28_000_000),
        name="update",
    )(
        neighbours, gap, received, from_below, from_above, face_speed, speed_picker(species, face_nodes),
        lift_picker(face_nodes), lift_operator.T, emission_profile.T, base, tile_rows,
    )

    theirs = lax.ppermute(for_other, "core", [(0, 1), (1, 0)])
    own = pl.pallas_call(
        own_kernel,
        in_specs=[vmem] * 2,
        out_specs=vmem,
        out_shape=sds((tiles // 2, width), F32),
        compiler_params=params(16),
        cost_estimate=cost(2_100_000_000, 2_000_000),
        name="scatter_own",
    )(tile_rows, contrib)
    partial = (own + theirs).astype(BF16)
    chips = groups * peers // 2
    pieces = lax.all_to_all(
        partial.reshape(chips, tiles // 2 // chips, width), ("z", "sub"), split_axis=0, concat_axis=0
    )
    emission_grad = jnp.sum(pieces.astype(F32), axis=0)
    return adjoint_next, emission_grad


def solution(mesh):
    groups, peers = mesh.devices.shape
    mesh = Mesh(mesh.devices.reshape(groups // 2, 2, peers), ("z", "core", "sub"))
    both = ("z", "core", "sub")
    placed = (
        P(None, None, both), P(None, None, both), P(None, both), P(), P(), P(),
        P(None, both), P(None, both), P(None, both), P(both), P(),
    )
    return jax.shard_map(
        on_device,
        mesh=mesh,
        in_specs=placed,
        out_specs=(P(None, None, both), P(both, None)),
        check_vma=False,
    )
```

```python
import functools

import jax
import jax.numpy as jnp
import numpy as np
from jax import lax
from jax.experimental import pallas as pl
from jax.experimental.pallas import tpu as pltpu
from jax.sharding import Mesh, PartitionSpec as P

ORDER = 5
SECTION = 0.125
MIB = 1024 * 1024
UPDATE_MIB = 46
MAIN = 32
REST = 4
GROUP_ROWS = 512
F32, BF16, I16, I32 = jnp.float32, jnp.bfloat16, jnp.int16, jnp.int32


def face_table(order):
    edge_nodes = order + 1
    coords_a, coords_b = np.meshgrid(np.arange(edge_nodes), np.arange(edge_nodes), indexing="ij")
    coords_a = coords_a.reshape(-1)
    coords_b = coords_b.reshape(-1)
    face_rows = []
    for axis_id in range(3):
        for level_id in (0, edge_nodes - 1):
            fixed_col = coords_a * 0 + level_id
            if axis_id == 0:
                triple = (fixed_col, coords_a, coords_b)
            elif axis_id == 1:
                triple = (coords_a, fixed_col, coords_b)
            else:
                triple = (coords_a, coords_b, fixed_col)
            face_rows.append((triple[0] * edge_nodes + triple[1]) * edge_nodes + triple[2])
    return np.stack(face_rows).astype(np.int32)


def picker(columns, lines):
    out = np.zeros((len(lines), columns), np.float32)
    for row, column in enumerate(lines):
        if column is not None:
            out[row, column] = 1.0
    return jnp.asarray(out, BF16)


def trace_picker(species, faces, first, last):
    table = face_table(ORDER)
    return jnp.stack([
        picker(last - first, [table[f, k] - first for f in faces for k in range(MAIN)] + [
            table[f, MAIN + j] - first if t == s else None
            for f in faces for t in range(species) for j in range(REST)
        ])
        for s in range(species)
    ])


def speed_picker(species, face_nodes):
    lines = [f * face_nodes + k for f in range(6) for k in range(MAIN)]
    lines += [f * face_nodes + MAIN + j for f in range(6) for _ in range(species) for j in range(REST)]
    return picker(6 * face_nodes, lines)


def lift_picker(face_nodes):
    lines = [f * face_nodes + k for f in range(6) for k in range(MAIN)]
    lines += [f * face_nodes + MAIN + j for f in range(6) for j in range(REST)]
    return picker(6 * face_nodes, lines)


def one_hot(count, positions):
    rows = lax.broadcasted_iota(I16, (count, positions.shape[1]), 0)
    return jnp.where(rows == positions.astype(I16), jnp.ones((), BF16), jnp.zeros((), BF16))


def dot(a, b):
    return jnp.dot(a, b, preferred_element_type=F32)


LOW, MID, HIGH = (0, 40), (40, 176), (176, 216)


def send_kernel(
    adj_hbm, near_hbm, far_hbm, ss_hbm, gs_hbm, pool_hbm, send_hbm, up_hbm, down_hbm,
    adj, near_ref, far_ref, ss_ref, gs_ref, pool_ref, send_ref, up_ref, down_ref, in_sems, pool_sems, out_sems,
):
    species = adj.shape[0]
    rows, elements = pool_ref.shape[1:]
    half = send_ref.shape[3] // 2
    pairs = [(near_hbm, near_ref), (ss_hbm, ss_ref)]
    pairs += [(adj_hbm.at[:, a:b, :], adj.at[:, a:b, :]) for a, b in (LOW, HIGH, MID)]
    pairs += [(far_hbm, far_ref), (gs_hbm, gs_ref)]
    copies = [pltpu.make_async_copy(x, y, in_sems.at[i]) for i, (x, y) in enumerate(pairs)]
    for copy in copies:
        copy.start()
    leaving = []

    def leave(source, target, sem):
        leaving.append(pltpu.make_async_copy(source, target, sem))
        leaving[-1].start()

    low = lax.broadcasted_iota(I32, (rows, 2 * half), 1) < half

    def exchange(q):
        a = dot(pool_ref[2 * q], one_hot(elements, ss_ref[2 * q : 2 * q + 1, :]))
        b = dot(pool_ref[2 * q + 1], one_hot(elements, ss_ref[2 * q + 1 : 2 * q + 2, :]))
        for i in range(send_ref.shape[0] // 2):
            lanes = slice(2 * half * i, 2 * half * (i + 1))
            ai, bi = a[:, lanes], b[:, lanes]
            send_ref[2 * i, q] = jnp.where(low, ai, pltpu.roll(bi, half, 1)).astype(BF16)
            send_ref[2 * i + 1, q] = jnp.where(low, pltpu.roll(ai, half, 1), bi).astype(BF16)

    def fill(faces, picks, first, last, chunk):
        count = len(faces)
        shared = species * REST
        for c in range(0, elements, chunk):
            found = [dot(picks[s], adj[s, first:last, c : c + chunk].astype(BF16)) for s in range(species)]
            rest = sum(x[MAIN * count :] for x in found)
            for i, f in enumerate(faces):
                pieces = [x[MAIN * i : MAIN * (i + 1)] for x in found] + [rest[shared * i : shared * (i + 1)]]
                pool_ref[f, :, c : c + chunk] = jnp.concatenate(pieces, axis=0).astype(BF16)

    for copy in copies[:4]:
        copy.wait()
    fill((0,), near_ref[0], *LOW, 1024)
    fill((1,), near_ref[1], *HIGH, 1024)
    exchange(0)
    leave(send_ref.at[:, 0], send_hbm.at[:, 0], out_sems.at[0])
    for f in (0, 1):
        leave(pool_ref.at[f], pool_hbm.at[f], pool_sems.at[f])
    for copy in copies[4:]:
        copy.wait()
    fill((2, 3, 4, 5), far_ref[...], 0, HIGH[1], 512)
    for f in (2, 3, 4, 5):
        leave(pool_ref.at[f], pool_hbm.at[f], pool_sems.at[f])
    down_ref[...] = dot(pool_ref[4], one_hot(elements, gs_ref[0:1, :])).astype(BF16)
    up_ref[...] = dot(pool_ref[5], one_hot(elements, gs_ref[1:2, :])).astype(BF16)
    exchange(1)
    leave(down_ref, down_hbm, out_sems.at[1])
    leave(up_ref, up_hbm, out_sems.at[2])
    leave(send_ref.at[:, 1], send_hbm.at[:, 1], out_sems.at[3])
    for copy in leaving:
        copy.wait()


def local_kernel(
    adj_hbm, vel_hbm, der_hbm, pool_hbm, nbr_ref, tile_ref, slot_ref, base_hbm, gap_hbm, row_ref,
    adj_all, vel_all, der, pool, mixed, gap_all, adj_sems, vel_sems, pool_sems, der_sem, base_sems, gap_sems,
):
    step = pl.program_id(0)
    steps, species, nodes, block = adj_all.shape
    group = 16

    def entering(index):
        cols = pl.ds(pl.multiple_of(index * block, block), block)
        return (
            pltpu.make_async_copy(adj_hbm.at[:, :, cols], adj_all.at[index], adj_sems.at[index]),
            pltpu.make_async_copy(vel_hbm.at[:, :, cols], vel_all.at[index], vel_sems.at[index]),
        )

    def base_leaving(index):
        return pltpu.make_async_copy(adj_all.at[index], base_hbm.at[index], base_sems.at[index])

    def gap_leaving(index, f):
        return pltpu.make_async_copy(gap_all.at[index, f], gap_hbm.at[index, f], gap_sems.at[index, f])

    matrix = pltpu.make_async_copy(der_hbm, der, der_sem.at[0])
    pools = [pltpu.make_async_copy(pool_hbm.at[f], pool.at[f], pool_sems.at[f]) for f in range(6)]

    @pl.when(step == 0)
    def _():
        matrix.start()
        for copy in (*entering(0), *pools):
            copy.start()
        for index in range(1, steps):
            for copy in entering(index):
                copy.start()
        tile_rows(tile_ref, slot_ref, row_ref, block)
        matrix.wait()
        for d in range(3):
            for b in range(nodes // group):
                rows = der[d * nodes + b * group : d * nodes + (b + 1) * group, :]
                mixed[(3 * b + d) * group : (3 * b + d + 1) * group, :] = rows * jnp.asarray(SECTION, BF16)

    for copy in entering(step):
        copy.wait()
    for s in range(species):
        g = dot(mixed[...], adj_all[step, s].astype(BF16))
        for b in range(nodes // group):
            rows = slice(b * group, (b + 1) * group)
            total = adj_all[step, s, rows]
            for d in range(3):
                total += vel_all[step, d, rows].astype(F32) * g[(3 * b + d) * group : (3 * b + d + 1) * group]
            adj_all[step, s, rows] = total
    base_leaving(step).start()

    @pl.when(step == 0)
    def _():
        for copy in pools:
            copy.wait()

    cols = pl.ds(pl.multiple_of(step * block, block), block)
    for f in range(6):
        hot = one_hot(pool.shape[2], nbr_ref[f : f + 1, cols])
        gap_all[step, f] = dot(pool[f ^ 1], hot) - pool[f, :, cols].astype(F32)
        gap_leaving(step, f).start()

    @pl.when(step == steps - 1)
    def _():
        for index in range(steps):
            base_leaving(index).wait()
            for f in range(6):
                gap_leaving(index, f).wait()


def tile_rows(tile_ref, slot_ref, row_ref, block):
    elements = tile_ref.shape[1]
    high, lanes = slot_ref.shape
    fine = lanes // 2
    slot = jnp.transpose(slot_ref[...].astype(F32))
    upper = jnp.floor(slot * (1.0 / 64.0))
    digits = jnp.concatenate([
        jnp.concatenate([x[:fine], x[fine:]], axis=1) for x in (upper, slot - 64.0 * upper)
    ], axis=0).astype(BF16)
    bits = fine.bit_length() - 1
    for c in range(0, elements, block):
        tile = tile_ref[:, c : c + block]
        coarse = jnp.right_shift(tile, bits)
        place = jnp.bitwise_and(coarse, 1) * high + jnp.right_shift(coarse, 1)
        found = dot(digits, one_hot(2 * high, place))
        rows = 64.0 * found[:fine] + found[fine:]
        within = lax.broadcasted_iota(I32, rows.shape, 0) == jnp.bitwise_and(tile, fine - 1)
        row_ref[:, c : c + block] = jnp.sum(jnp.where(within, rows, 0.0), axis=0, keepdims=True).astype(I32)


def update_kernel(
    nbr_ref, gap_hbm, recv_ref, below_ref, above_ref, fs_ref, speed_ref, order_ref, lift_ref, prof_ref, base_hbm, row_hbm,
    next_hbm, contrib_ref, other_ref, seen_ref, rpool, lift_sorted, flux, low_next, gap_all, base_all, row_ref,
    sems, next_sems, row_sem, *, elements,
):
    step = pl.program_id(0)
    peers, _, rows, width = recv_ref.shape
    half = width // 2
    steps, species, nodes, block = base_all.shape

    def loads(index):
        return (
            pltpu.make_async_copy(gap_hbm.at[index], gap_all.at[index], sems.at[0, index]),
            pltpu.make_async_copy(base_hbm.at[index], base_all.at[index], sems.at[1, index]),
        )

    def leaving(index):
        cols = pl.ds(pl.multiple_of(index * block, block), block)
        return pltpu.make_async_copy(base_all.at[index], next_hbm.at[:, :, cols], next_sems.at[index])

    lines = pltpu.make_async_copy(row_hbm, row_ref, row_sem.at[0])

    def contribute(index):
        terms = [dot(prof_ref[...], low_next[s]) for s in range(species)]
        contrib = jnp.transpose(jnp.concatenate(terms, axis=0))
        high = contrib.astype(BF16)
        lines = pl.ds(pl.multiple_of(index * block, block), block)
        contrib_ref[lines, : contrib.shape[1]] = high
        contrib_ref[lines, contrib.shape[1] :] = (contrib - high.astype(F32)).astype(BF16)

    @pl.when(step == 0)
    def _():
        for index in range(steps):
            for copy in loads(index):
                copy.start()
        lines.start()
        low = lax.broadcasted_iota(I32, (rows, width), 1) < half
        for q in range(2):
            for i in range(peers // 2):
                lanes = slice(width * i, width * (i + 1))
                x = recv_ref[2 * i, q].astype(F32)
                y = recv_ref[2 * i + 1, q].astype(F32)
                rpool[2 * q, :, lanes] = jnp.where(low, x, pltpu.roll(y, half, 1)).astype(BF16)
                rpool[2 * q + 1, :, lanes] = jnp.where(low, pltpu.roll(x, half, 1), y).astype(BF16)
        lift_sorted[...] = (SECTION * jnp.transpose(dot(order_ref[...], lift_ref[...]))).astype(BF16)
        low_next[...] = jnp.zeros_like(low_next)

    for copy in loads(step):
        copy.wait()
    gap_ref, base_ref = gap_all.at[step], base_all.at[step]
    contribute(jnp.maximum(step - 1, 0))
    upwind = dot(speed_ref[...], jnp.maximum(fs_ref[...], jnp.zeros((), BF16)))
    slots = peers * half
    first = lax.broadcasted_iota(I32, (2 * REST, block), 0) < REST
    tails = [[] for _ in range(species)]
    for q in range(3):
        mains, rests = [], []
        for f in (2 * q, 2 * q + 1):
            t = f ^ 1
            if t < 4:
                far = dot(rpool[t], one_hot(slots, nbr_ref[f : f + 1, :] - elements))
            else:
                source = below_ref if t == 5 else above_ref
                hot = one_hot(source.shape[1], nbr_ref[f : f + 1, :] - (elements + slots))
                far = dot(source[...], hot)
            gap = gap_ref[f] + far
            speed = upwind[MAIN * f : MAIN * (f + 1)]
            mains.append([speed * gap[MAIN * s : MAIN * (s + 1)] for s in range(species)])
            line = 6 * MAIN + species * REST * f
            rests.append(upwind[line : line + species * REST] * gap[species * MAIN :])
        for s in range(species):
            both = jnp.concatenate([mains[0][s], mains[1][s]], axis=0).astype(BF16)
            flux[s, 2 * MAIN * q : 2 * MAIN * (q + 1), :] = both
        for v in range(species // 2):
            a = rests[0][2 * REST * v : 2 * REST * (v + 1)]
            b = rests[1][2 * REST * v : 2 * REST * (v + 1)]
            tails[2 * v].append(jnp.where(first, a, pltpu.roll(b, REST, 0)))
            tails[2 * v + 1].append(jnp.where(first, pltpu.roll(a, REST, 0), b))
    for s in range(species):
        flux[s, 6 * MAIN :, :] = jnp.concatenate(tails[s], axis=0).astype(BF16)
    for s in range(species):
        value = base_ref[s] + dot(lift_sorted[...], flux[s])
        base_ref[s] = value
        low_next[s] = value.astype(BF16)
    leaving(step).start()

    @pl.when(step == steps - 1)
    def _():
        contribute(step)
        lines.wait()
        seen_ref[...] = row_ref[...]
        scatter(row_ref, contrib_ref, other_ref, True)
        for index in range(steps):
            leaving(index).wait()


def scatter(row_ref, contrib_ref, out_ref, other):
    width = out_ref.shape[1]
    core = lax.axis_index("core")
    side = 1 - core if other else core
    for i in range(out_ref.shape[0] // GROUP_ROWS):
        hot = one_hot(GROUP_ROWS, row_ref[...] - (2 * i + side) * GROUP_ROWS)
        both = dot(hot, contrib_ref[...])
        out_ref[i * GROUP_ROWS : (i + 1) * GROUP_ROWS, :] = both[:, :width] + both[:, width:]


def own_kernel(row_ref, contrib_ref, out_ref):
    scatter(row_ref, contrib_ref, out_ref, False)


def whole(*shape):
    return pl.BlockSpec(shape, lambda i: (0,) * len(shape))


def params(mib):
    return pltpu.CompilerParams(vmem_limit_bytes=mib * MIB)


def cost(flops, nbytes):
    return pl.CostEstimate(flops=flops, bytes_accessed=nbytes, transcendentals=0)


def on_device(
    adjoint, velocity, face_speed, derivatives, lift_operator, emission_profile,
    neighbours, sub_sends, group_sends, element_tile, tile_slot,
):
    species, nodes, elements = adjoint.shape
    peers = lax.axis_size("sub")
    groups = lax.axis_size("z") * lax.axis_size("core")
    slots = sub_sends.shape[1]
    half = slots // peers
    vcap = group_sends.shape[1]
    tiles = tile_slot.shape[0]
    heights = emission_profile.shape[1]
    face_rows = face_speed.shape[0]
    rows = species * (MAIN + REST)
    sds = jax.ShapeDtypeStruct
    block = 512
    steps = elements // block

    near = jnp.stack([trace_picker(species, (f,), *span) for f, span in enumerate((LOW, HIGH))])
    far = trace_picker(species, (2, 3, 4, 5), 0, HIGH[1])
    vmem = pl.BlockSpec(memory_space=pltpu.VMEM)
    hbm = pl.BlockSpec(memory_space=pltpu.HBM)
    made = [
        sds((6, rows, elements), BF16), sds((peers, 2, rows, 2 * half), BF16), sds((rows, vcap), BF16), sds((rows, vcap), BF16),
    ]
    pool, send, up, down = pl.pallas_call(
        send_kernel,
        in_specs=[hbm] * 5,
        out_specs=[hbm] * 4,
        out_shape=made,
        scratch_shapes=[
            pltpu.VMEM((species, HIGH[1], elements), F32),
            *(pltpu.VMEM(x.shape, x.dtype) for x in (near, far, sub_sends, group_sends, *made)),
            pltpu.SemaphoreType.DMA((7,)), pltpu.SemaphoreType.DMA((6,)), pltpu.SemaphoreType.DMA((4,)),
        ],
        compiler_params=params(60),
        cost_estimate=cost(12_000_000_000, 14_000_000),
        name="sends",
    )(
        adjoint, near, far, sub_sends, group_sends,
    )

    received = lax.all_to_all(send, "sub", split_axis=0, concat_axis=0, tiled=True)
    ring_up = [(g, (g + 1) % groups) for g in range(groups)]
    ring_down = [(g, (g - 1) % groups) for g in range(groups)]
    from_below = lax.ppermute(up, ("z", "core"), ring_up)
    from_above = lax.ppermute(down, ("z", "core"), ring_down)

    base, gap, tile_row = pl.pallas_call(
        local_kernel,
        grid=(steps,),
        in_specs=[hbm] * 4 + [whole(6, elements), whole(1, elements), whole(tiles // 128, 128)],
        out_specs=[hbm, hbm, whole(1, elements)],
        out_shape=[
            sds((steps, species, nodes, block), F32), sds((steps, 6, rows, block), F32), sds((1, elements), I32),
        ],
        scratch_shapes=[
            pltpu.VMEM((steps, species, nodes, block), F32), pltpu.VMEM((steps, 3, nodes, block), BF16),
            pltpu.VMEM((3 * nodes, nodes), BF16), pltpu.VMEM((6, rows, elements), BF16),
            pltpu.VMEM((3 * nodes, nodes), BF16), pltpu.VMEM((steps, 6, rows, block), F32),
            *(pltpu.SemaphoreType.DMA(shape) for shape in ((steps,), (steps,), (6,), (1,), (steps,), (steps, 6))),
        ],
        compiler_params=params(60),
        cost_estimate=cost(16_000_000_000, 32_000_000),
        name="local",
    )(
        adjoint, velocity, derivatives, pool, neighbours, element_tile.reshape(1, elements),
        tile_slot.reshape(tiles // 128, 128),
    )

    face_nodes = face_rows // 6
    width = species * heights
    adjoint_next, contrib, for_other, seen_row = pl.pallas_call(
        functools.partial(update_kernel, elements=elements),
        grid=(steps,),
        in_specs=[
            pl.BlockSpec((6, block), lambda i: (0, i)),
            hbm, whole(peers, 2, rows, 2 * half), whole(rows, vcap), whole(rows, vcap),
            pl.BlockSpec((face_rows, block), lambda i: (0, i)),
            whole(2 * rows, face_rows), whole(face_rows, face_rows), whole(face_rows, nodes), whole(heights, nodes),
            hbm, hbm,
        ],
        out_specs=[
            hbm, whole(elements, 2 * width), whole(tiles // 2, width), whole(1, elements),
        ],
        out_shape=[
            sds((species, nodes, elements), F32), sds((elements, 2 * width), BF16), sds((tiles // 2, width), F32),
            sds((1, elements), I32),
        ],
        scratch_shapes=[
            pltpu.VMEM((4, rows, slots), BF16), pltpu.VMEM((nodes, face_rows), BF16),
            pltpu.VMEM((species, face_rows, block), BF16), pltpu.VMEM((species, nodes, block), BF16),
            pltpu.VMEM((steps, 6, rows, block), F32), pltpu.VMEM((steps, species, nodes, block), F32),
            pltpu.VMEM((1, elements), I32),
            pltpu.SemaphoreType.DMA((2, steps)), pltpu.SemaphoreType.DMA((steps,)), pltpu.SemaphoreType.DMA((1,)),
        ],
        compiler_params=params(UPDATE_MIB),
        cost_estimate=cost(8_000_000_000, 28_000_000),
        name="update",
    )(
        neighbours, gap, received, from_below, from_above, face_speed, speed_picker(species, face_nodes),
        lift_picker(face_nodes), lift_operator.T, emission_profile.T, base, tile_row,
    )

    theirs = lax.ppermute(for_other, "core", [(0, 1), (1, 0)])
    own = pl.pallas_call(
        own_kernel,
        in_specs=[vmem] * 2,
        out_specs=vmem,
        out_shape=sds((tiles // 2, width), F32),
        compiler_params=params(16),
        cost_estimate=cost(2_100_000_000, 2_000_000),
        name="scatter_own",
    )(seen_row, contrib)
    partial = (own + theirs).astype(BF16)
    chips = groups * peers // 2
    pieces = lax.all_to_all(
        partial.reshape(chips, tiles // 2 // chips, width), ("z", "sub"), split_axis=0, concat_axis=0
    )
    emission_grad = jnp.sum(pieces.astype(F32), axis=0)
    return adjoint_next, emission_grad


def solution(mesh):
    groups, peers = mesh.devices.shape
    mesh = Mesh(mesh.devices.reshape(groups // 2, 2, peers), ("z", "core", "sub"))
    both = ("z", "core", "sub")
    placed = (
        P(None, None, both), P(None, None, both), P(None, both), P(), P(), P(),
        P(None, both), P(None, both), P(None, both), P(both), P(),
    )
    return jax.shard_map(
        on_device,
        mesh=mesh,
        in_specs=placed,
        out_specs=(P(None, None, both), P(both, None)),
        check_vma=False,
    )
```

```python
import functools

import jax
import jax.numpy as jnp
import numpy as np
from jax import lax
from jax.experimental import pallas as pl
from jax.experimental.pallas import tpu as pltpu
from jax.sharding import Mesh, PartitionSpec as P

ORDER = 5
SECTION = 0.125
MIB = 1024 * 1024
UPDATE_MIB = 46
MAIN = 32
REST = 4
GROUP_ROWS = 512
F32, BF16, I16, I32 = jnp.float32, jnp.bfloat16, jnp.int16, jnp.int32


def face_table(order):
    edge_nodes = order + 1
    coords_a, coords_b = np.meshgrid(np.arange(edge_nodes), np.arange(edge_nodes), indexing="ij")
    coords_a = coords_a.reshape(-1)
    coords_b = coords_b.reshape(-1)
    face_rows = []
    for axis_id in range(3):
        for level_id in (0, edge_nodes - 1):
            fixed_col = coords_a * 0 + level_id
            if axis_id == 0:
                triple = (fixed_col, coords_a, coords_b)
            elif axis_id == 1:
                triple = (coords_a, fixed_col, coords_b)
            else:
                triple = (coords_a, coords_b, fixed_col)
            face_rows.append((triple[0] * edge_nodes + triple[1]) * edge_nodes + triple[2])
    return np.stack(face_rows).astype(np.int32)


def picker(columns, lines):
    out = np.zeros((len(lines), columns), np.float32)
    for row, column in enumerate(lines):
        if column is not None:
            out[row, column] = 1.0
    return jnp.asarray(out, BF16)


def trace_picker(species, faces, first, last):
    table = face_table(ORDER)
    return jnp.stack([
        picker(last - first, [table[f, k] - first for f in faces for k in range(MAIN)] + [
            table[f, MAIN + j] - first if t == s else None
            for f in faces for t in range(species) for j in range(REST)
        ])
        for s in range(species)
    ])


def speed_picker(species, face_nodes):
    lines = [f * face_nodes + k for f in range(6) for k in range(MAIN)]
    lines += [f * face_nodes + MAIN + j for f in range(6) for _ in range(species) for j in range(REST)]
    return picker(6 * face_nodes, lines)


def lift_picker(face_nodes):
    lines = [f * face_nodes + k for f in range(6) for k in range(MAIN)]
    lines += [f * face_nodes + MAIN + j for f in range(6) for j in range(REST)]
    return picker(6 * face_nodes, lines)


def one_hot(count, positions):
    rows = lax.broadcasted_iota(I16, (count, positions.shape[1]), 0)
    return jnp.where(rows == positions.astype(I16), jnp.ones((), BF16), jnp.zeros((), BF16))


def dot(a, b):
    return jnp.dot(a, b, preferred_element_type=F32)


LOW, MID, HIGH = (0, 40), (40, 176), (176, 216)


def send_kernel(
    adj_hbm, near_hbm, far_hbm, ss_hbm, gs_hbm, pool_hbm, send_hbm, up_hbm, down_hbm,
    adj, near_ref, far_ref, ss_ref, gs_ref, pool_ref, send_ref, up_ref, down_ref, in_sems, pool_sems, out_sems,
):
    species = adj.shape[0]
    rows, elements = pool_ref.shape[1:]
    half = send_ref.shape[3] // 2
    pairs = [(near_hbm, near_ref), (ss_hbm, ss_ref)]
    pairs += [(adj_hbm.at[:, a:b, :], adj.at[:, a:b, :]) for a, b in (LOW, HIGH, MID)]
    pairs += [(far_hbm, far_ref), (gs_hbm, gs_ref)]
    copies = [pltpu.make_async_copy(x, y, in_sems.at[i]) for i, (x, y) in enumerate(pairs)]
    for copy in copies:
        copy.start()
    leaving = []

    def leave(source, target, sem):
        leaving.append(pltpu.make_async_copy(source, target, sem))
        leaving[-1].start()

    low = lax.broadcasted_iota(I32, (rows, 2 * half), 1) < half

    def exchange(q):
        a = dot(pool_ref[2 * q], one_hot(elements, ss_ref[2 * q : 2 * q + 1, :]))
        b = dot(pool_ref[2 * q + 1], one_hot(elements, ss_ref[2 * q + 1 : 2 * q + 2, :]))
        for i in range(send_ref.shape[0] // 2):
            lanes = slice(2 * half * i, 2 * half * (i + 1))
            ai, bi = a[:, lanes], b[:, lanes]
            send_ref[2 * i, q] = jnp.where(low, ai, pltpu.roll(bi, half, 1)).astype(BF16)
            send_ref[2 * i + 1, q] = jnp.where(low, pltpu.roll(ai, half, 1), bi).astype(BF16)

    def fill(faces, picks, first, last, chunk):
        count = len(faces)
        shared = species * REST
        for c in range(0, elements, chunk):
            found = [dot(picks[s], adj[s, first:last, c : c + chunk].astype(BF16)) for s in range(species)]
            rest = sum(x[MAIN * count :] for x in found)
            for i, f in enumerate(faces):
                pieces = [x[MAIN * i : MAIN * (i + 1)] for x in found] + [rest[shared * i : shared * (i + 1)]]
                pool_ref[f, :, c : c + chunk] = jnp.concatenate(pieces, axis=0).astype(BF16)

    for copy in copies[:4]:
        copy.wait()
    fill((0,), near_ref[0], *LOW, 1024)
    fill((1,), near_ref[1], *HIGH, 1024)
    exchange(0)
    leave(send_ref.at[:, 0], send_hbm.at[:, 0], out_sems.at[0])
    for f in (0, 1):
        leave(pool_ref.at[f], pool_hbm.at[f], pool_sems.at[f])
    for copy in copies[4:]:
        copy.wait()
    fill((2, 3, 4, 5), far_ref[...], 0, HIGH[1], 512)
    for f in (2, 3, 4, 5):
        leave(pool_ref.at[f], pool_hbm.at[f], pool_sems.at[f])
    down_ref[...] = dot(pool_ref[4], one_hot(elements, gs_ref[0:1, :])).astype(BF16)
    up_ref[...] = dot(pool_ref[5], one_hot(elements, gs_ref[1:2, :])).astype(BF16)
    exchange(1)
    leave(down_ref, down_hbm, out_sems.at[1])
    leave(up_ref, up_hbm, out_sems.at[2])
    leave(send_ref.at[:, 1], send_hbm.at[:, 1], out_sems.at[3])
    for copy in leaving:
        copy.wait()


def local_kernel(
    adj_ref, vel_ref, der_ref, nbr_ref, pool_hbm, tile_ref, slot_ref, base_ref, gap_ref, pool, mixed, digits, sems,
):
    step = pl.program_id(0)
    species, nodes, block = adj_ref.shape
    rows = pool.shape[1]
    group = 16
    copies = [pltpu.make_async_copy(pool_hbm.at[f], pool.at[f], sems.at[f]) for f in range(6)]

    @pl.when(step == 0)
    def _():
        for copy in copies:
            copy.start()
        for d in range(3):
            for b in range(nodes // group):
                lines = der_ref[d * nodes + b * group : d * nodes + (b + 1) * group, :]
                mixed[(3 * b + d) * group : (3 * b + d + 1) * group, :] = lines * jnp.asarray(SECTION, BF16)
        digits[...] = slot_digits(slot_ref)

    for s in range(species):
        g = dot(mixed[...], adj_ref[s].astype(BF16))
        for b in range(nodes // group):
            lines = slice(b * group, (b + 1) * group)
            total = adj_ref[s, lines]
            for d in range(3):
                total += vel_ref[d, lines].astype(F32) * g[(3 * b + d) * group : (3 * b + d + 1) * group]
            base_ref[0, s, lines] = total
    gap_ref[0, 6 * rows :] = tile_rows(tile_ref[...], digits[...])

    @pl.when(step == 0)
    def _():
        for copy in copies:
            copy.wait()

    cols = pl.ds(pl.multiple_of(step * block, block), block)
    for f in range(6):
        hot = one_hot(pool.shape[2], nbr_ref[f : f + 1, :])
        gap_ref[0, rows * f : rows * (f + 1)] = dot(pool[f ^ 1], hot) - pool[f, :, cols].astype(F32)


def slot_digits(slot_ref):
    fine = slot_ref.shape[1] // 2
    slot = jnp.transpose(slot_ref[...].astype(F32))
    upper = jnp.floor(slot * (1.0 / 64.0))
    return jnp.concatenate([
        jnp.concatenate([x[:fine], x[fine:]], axis=1) for x in (upper, slot - 64.0 * upper)
    ], axis=0).astype(BF16)


def tile_rows(tile, digits):
    fine, high = digits.shape[0] // 2, digits.shape[1] // 2
    coarse = jnp.right_shift(tile, fine.bit_length() - 1)
    place = jnp.bitwise_and(coarse, 1) * high + jnp.right_shift(coarse, 1)
    found = dot(digits, one_hot(2 * high, place))
    rows = 64.0 * found[:fine] + found[fine:]
    within = lax.broadcasted_iota(I32, rows.shape, 0) == jnp.bitwise_and(tile, fine - 1)
    return jnp.broadcast_to(jnp.sum(jnp.where(within, rows, 0.0), axis=0, keepdims=True), (8, tile.shape[1]))


def update_kernel(
    nbr_ref, gap_hbm, recv_ref, below_ref, above_ref, fs_ref, speed_ref, order_ref, lift_ref, prof_ref, base_hbm,
    next_hbm, contrib_ref, other_ref, seen_ref, rpool, lift_sorted, flux, low_next, gap_all, base_all, row_ref,
    sems, next_sems, *, elements,
):
    step = pl.program_id(0)
    peers, _, rows, width = recv_ref.shape
    half = width // 2
    steps, species, nodes, block = base_all.shape

    def loads(index):
        return (
            pltpu.make_async_copy(gap_hbm.at[index], gap_all.at[index], sems.at[0, index]),
            pltpu.make_async_copy(base_hbm.at[index], base_all.at[index], sems.at[1, index]),
        )

    def leaving(index):
        cols = pl.ds(pl.multiple_of(index * block, block), block)
        return pltpu.make_async_copy(base_all.at[index], next_hbm.at[:, :, cols], next_sems.at[index])

    def contribute(index):
        terms = [dot(prof_ref[...], low_next[s]) for s in range(species)]
        contrib = jnp.transpose(jnp.concatenate(terms, axis=0))
        high = contrib.astype(BF16)
        lines = pl.ds(pl.multiple_of(index * block, block), block)
        contrib_ref[lines, : contrib.shape[1]] = high
        contrib_ref[lines, contrib.shape[1] :] = (contrib - high.astype(F32)).astype(BF16)

    @pl.when(step == 0)
    def _():
        for index in range(steps):
            for copy in loads(index):
                copy.start()
        low = lax.broadcasted_iota(I32, (rows, width), 1) < half
        for q in range(2):
            for i in range(peers // 2):
                lanes = slice(width * i, width * (i + 1))
                x = recv_ref[2 * i, q].astype(F32)
                y = recv_ref[2 * i + 1, q].astype(F32)
                rpool[2 * q, :, lanes] = jnp.where(low, x, pltpu.roll(y, half, 1)).astype(BF16)
                rpool[2 * q + 1, :, lanes] = jnp.where(low, pltpu.roll(x, half, 1), y).astype(BF16)
        lift_sorted[...] = (SECTION * jnp.transpose(dot(order_ref[...], lift_ref[...]))).astype(BF16)
        low_next[...] = jnp.zeros_like(low_next)

    for copy in loads(step):
        copy.wait()
    gap_ref, base_ref = gap_all.at[step], base_all.at[step]
    row_ref[:, pl.ds(pl.multiple_of(step * block, block), block)] = gap_ref[6 * rows : 6 * rows + 1].astype(I32)
    contribute(jnp.maximum(step - 1, 0))
    upwind = dot(speed_ref[...], jnp.maximum(fs_ref[...], jnp.zeros((), BF16)))
    slots = peers * half
    first = lax.broadcasted_iota(I32, (2 * REST, block), 0) < REST
    tails = [[] for _ in range(species)]
    for q in range(3):
        mains, rests = [], []
        for f in (2 * q, 2 * q + 1):
            t = f ^ 1
            if t < 4:
                far = dot(rpool[t], one_hot(slots, nbr_ref[f : f + 1, :] - elements))
            else:
                source = below_ref if t == 5 else above_ref
                hot = one_hot(source.shape[1], nbr_ref[f : f + 1, :] - (elements + slots))
                far = dot(source[...], hot)
            gap = gap_ref[rows * f : rows * (f + 1)] + far
            speed = upwind[MAIN * f : MAIN * (f + 1)]
            mains.append([speed * gap[MAIN * s : MAIN * (s + 1)] for s in range(species)])
            line = 6 * MAIN + species * REST * f
            rests.append(upwind[line : line + species * REST] * gap[species * MAIN :])
        for s in range(species):
            both = jnp.concatenate([mains[0][s], mains[1][s]], axis=0).astype(BF16)
            flux[s, 2 * MAIN * q : 2 * MAIN * (q + 1), :] = both
        for v in range(species // 2):
            a = rests[0][2 * REST * v : 2 * REST * (v + 1)]
            b = rests[1][2 * REST * v : 2 * REST * (v + 1)]
            tails[2 * v].append(jnp.where(first, a, pltpu.roll(b, REST, 0)))
            tails[2 * v + 1].append(jnp.where(first, pltpu.roll(a, REST, 0), b))
    for s in range(species):
        flux[s, 6 * MAIN :, :] = jnp.concatenate(tails[s], axis=0).astype(BF16)
    for s in range(species):
        value = base_ref[s] + dot(lift_sorted[...], flux[s])
        base_ref[s] = value
        low_next[s] = value.astype(BF16)
    leaving(step).start()

    @pl.when(step == steps - 1)
    def _():
        contribute(step)
        seen_ref[...] = row_ref[...]
        scatter(row_ref, contrib_ref, other_ref, True)
        for index in range(steps):
            leaving(index).wait()


def scatter(row_ref, contrib_ref, out_ref, other):
    width = out_ref.shape[1]
    core = lax.axis_index("core")
    side = 1 - core if other else core
    for i in range(out_ref.shape[0] // GROUP_ROWS):
        hot = one_hot(GROUP_ROWS, row_ref[...] - (2 * i + side) * GROUP_ROWS)
        both = dot(hot, contrib_ref[...])
        out_ref[i * GROUP_ROWS : (i + 1) * GROUP_ROWS, :] = both[:, :width] + both[:, width:]


def own_kernel(row_ref, contrib_ref, out_ref):
    scatter(row_ref, contrib_ref, out_ref, False)


def whole(*shape):
    return pl.BlockSpec(shape, lambda i: (0,) * len(shape))


def params(mib):
    return pltpu.CompilerParams(vmem_limit_bytes=mib * MIB)


def cost(flops, nbytes):
    return pl.CostEstimate(flops=flops, bytes_accessed=nbytes, transcendentals=0)


def on_device(
    adjoint, velocity, face_speed, derivatives, lift_operator, emission_profile,
    neighbours, sub_sends, group_sends, element_tile, tile_slot,
):
    species, nodes, elements = adjoint.shape
    peers = lax.axis_size("sub")
    groups = lax.axis_size("z") * lax.axis_size("core")
    slots = sub_sends.shape[1]
    half = slots // peers
    vcap = group_sends.shape[1]
    tiles = tile_slot.shape[0]
    heights = emission_profile.shape[1]
    face_rows = face_speed.shape[0]
    rows = species * (MAIN + REST)
    sds = jax.ShapeDtypeStruct
    block = 512
    steps = elements // block

    near = jnp.stack([trace_picker(species, (f,), *span) for f, span in enumerate((LOW, HIGH))])
    far = trace_picker(species, (2, 3, 4, 5), 0, HIGH[1])
    vmem = pl.BlockSpec(memory_space=pltpu.VMEM)
    hbm = pl.BlockSpec(memory_space=pltpu.HBM)
    made = [
        sds((6, rows, elements), BF16), sds((peers, 2, rows, 2 * half), BF16), sds((rows, vcap), BF16), sds((rows, vcap), BF16),
    ]
    pool, send, up, down = pl.pallas_call(
        send_kernel,
        in_specs=[hbm] * 5,
        out_specs=[hbm] * 4,
        out_shape=made,
        scratch_shapes=[
            pltpu.VMEM((species, HIGH[1], elements), F32),
            *(pltpu.VMEM(x.shape, x.dtype) for x in (near, far, sub_sends, group_sends, *made)),
            pltpu.SemaphoreType.DMA((7,)), pltpu.SemaphoreType.DMA((6,)), pltpu.SemaphoreType.DMA((4,)),
        ],
        compiler_params=params(60),
        cost_estimate=cost(12_000_000_000, 14_000_000),
        name="sends",
    )(
        adjoint, near, far, sub_sends, group_sends,
    )

    received = lax.all_to_all(send, "sub", split_axis=0, concat_axis=0, tiled=True)
    ring_up = [(g, (g + 1) % groups) for g in range(groups)]
    ring_down = [(g, (g - 1) % groups) for g in range(groups)]
    from_below = lax.ppermute(up, ("z", "core"), ring_up)
    from_above = lax.ppermute(down, ("z", "core"), ring_down)

    base, gap = pl.pallas_call(
        local_kernel,
        grid=(steps,),
        in_specs=[
            pl.BlockSpec((species, nodes, block), lambda i: (0, 0, i)),
            pl.BlockSpec((3, nodes, block), lambda i: (0, 0, i)),
            whole(3 * nodes, nodes),
            pl.BlockSpec((6, block), lambda i: (0, i)),
            hbm,
            pl.BlockSpec((1, block), lambda i: (0, i)), whole(tiles // 128, 128),
        ],
        out_specs=[
            pl.BlockSpec((1, species, nodes, block), lambda i: (i, 0, 0, 0)),
            pl.BlockSpec((1, 6 * rows + 8, block), lambda i: (i, 0, 0)),
        ],
        out_shape=[sds((steps, species, nodes, block), F32), sds((steps, 6 * rows + 8, block), F32)],
        scratch_shapes=[
            pltpu.VMEM((6, rows, elements), BF16), pltpu.VMEM((3 * nodes, nodes), BF16),
            pltpu.VMEM((128, 2 * tiles // 128), BF16), pltpu.SemaphoreType.DMA((6,)),
        ],
        compiler_params=params(60),
        cost_estimate=cost(16_000_000_000, 32_000_000),
        name="local",
    )(
        adjoint, velocity, derivatives, neighbours, pool, element_tile.reshape(1, elements),
        tile_slot.reshape(tiles // 128, 128),
    )

    face_nodes = face_rows // 6
    width = species * heights
    adjoint_next, contrib, for_other, seen_row = pl.pallas_call(
        functools.partial(update_kernel, elements=elements),
        grid=(steps,),
        in_specs=[
            pl.BlockSpec((6, block), lambda i: (0, i)),
            hbm, whole(peers, 2, rows, 2 * half), whole(rows, vcap), whole(rows, vcap),
            pl.BlockSpec((face_rows, block), lambda i: (0, i)),
            whole(2 * rows, face_rows), whole(face_rows, face_rows), whole(face_rows, nodes), whole(heights, nodes),
            hbm,
        ],
        out_specs=[
            hbm, whole(elements, 2 * width), whole(tiles // 2, width), whole(1, elements),
        ],
        out_shape=[
            sds((species, nodes, elements), F32), sds((elements, 2 * width), BF16), sds((tiles // 2, width), F32),
            sds((1, elements), I32),
        ],
        scratch_shapes=[
            pltpu.VMEM((4, rows, slots), BF16), pltpu.VMEM((nodes, face_rows), BF16),
            pltpu.VMEM((species, face_rows, block), BF16), pltpu.VMEM((species, nodes, block), BF16),
            pltpu.VMEM((steps, 6 * rows + 8, block), F32), pltpu.VMEM((steps, species, nodes, block), F32),
            pltpu.VMEM((1, elements), I32),
            pltpu.SemaphoreType.DMA((2, steps)), pltpu.SemaphoreType.DMA((steps,)),
        ],
        compiler_params=params(UPDATE_MIB),
        cost_estimate=cost(8_000_000_000, 28_000_000),
        name="update",
    )(
        neighbours, gap, received, from_below, from_above, face_speed, speed_picker(species, face_nodes),
        lift_picker(face_nodes), lift_operator.T, emission_profile.T, base,
    )

    theirs = lax.ppermute(for_other, "core", [(0, 1), (1, 0)])
    own = pl.pallas_call(
        own_kernel,
        in_specs=[vmem] * 2,
        out_specs=vmem,
        out_shape=sds((tiles // 2, width), F32),
        compiler_params=params(16),
        cost_estimate=cost(2_100_000_000, 2_000_000),
        name="scatter_own",
    )(seen_row, contrib)
    partial = (own + theirs).astype(BF16)
    chips = groups * peers // 2
    pieces = lax.all_to_all(
        partial.reshape(chips, tiles // 2 // chips, width), ("z", "sub"), split_axis=0, concat_axis=0
    )
    emission_grad = jnp.sum(pieces.astype(F32), axis=0)
    return adjoint_next, emission_grad


def solution(mesh):
    groups, peers = mesh.devices.shape
    mesh = Mesh(mesh.devices.reshape(groups // 2, 2, peers), ("z", "core", "sub"))
    both = ("z", "core", "sub")
    placed = (
        P(None, None, both), P(None, None, both), P(None, both), P(), P(), P(),
        P(None, both), P(None, both), P(None, both), P(both), P(),
    )
    return jax.shard_map(
        on_device,
        mesh=mesh,
        in_specs=placed,
        out_specs=(P(None, None, both), P(both, None)),
        check_vma=False,
    )
```

```python
import functools

import jax
import jax.numpy as jnp
import numpy as np
from jax import lax
from jax.experimental import pallas as pl
from jax.experimental.pallas import tpu as pltpu
from jax.sharding import Mesh, PartitionSpec as P

ORDER = 5
SECTION = 0.125
MIB = 1024 * 1024
UPDATE_MIB = 46
MAIN = 32
REST = 4
GROUP_ROWS = 512
F32, BF16, I16, I32 = jnp.float32, jnp.bfloat16, jnp.int16, jnp.int32


def face_table(order):
    edge_nodes = order + 1
    coords_a, coords_b = np.meshgrid(np.arange(edge_nodes), np.arange(edge_nodes), indexing="ij")
    coords_a = coords_a.reshape(-1)
    coords_b = coords_b.reshape(-1)
    face_rows = []
    for axis_id in range(3):
        for level_id in (0, edge_nodes - 1):
            fixed_col = coords_a * 0 + level_id
            if axis_id == 0:
                triple = (fixed_col, coords_a, coords_b)
            elif axis_id == 1:
                triple = (coords_a, fixed_col, coords_b)
            else:
                triple = (coords_a, coords_b, fixed_col)
            face_rows.append((triple[0] * edge_nodes + triple[1]) * edge_nodes + triple[2])
    return np.stack(face_rows).astype(np.int32)


def picker(columns, lines):
    out = np.zeros((len(lines), columns), np.float32)
    for row, column in enumerate(lines):
        if column is not None:
            out[row, column] = 1.0
    return jnp.asarray(out, BF16)


def trace_picker(species, faces, first, last):
    table = face_table(ORDER)
    return jnp.stack([
        picker(last - first, [table[f, k] - first for f in faces for k in range(MAIN)] + [
            table[f, MAIN + j] - first if t == s else None
            for f in faces for t in range(species) for j in range(REST)
        ])
        for s in range(species)
    ])


def speed_picker(species, face_nodes):
    lines = [f * face_nodes + k for f in range(6) for k in range(MAIN)]
    lines += [f * face_nodes + MAIN + j for f in range(6) for _ in range(species) for j in range(REST)]
    return picker(6 * face_nodes, lines)


def lift_picker(face_nodes):
    lines = [f * face_nodes + k for f in range(6) for k in range(MAIN)]
    lines += [f * face_nodes + MAIN + j for f in range(6) for j in range(REST)]
    return picker(6 * face_nodes, lines)


def one_hot(count, positions):
    rows = lax.broadcasted_iota(I16, (count, positions.shape[1]), 0)
    return jnp.where(rows == positions.astype(I16), jnp.ones((), BF16), jnp.zeros((), BF16))


def dot(a, b):
    return jnp.dot(a, b, preferred_element_type=F32)


LOW, MID, HIGH = (0, 40), (40, 176), (176, 216)


def send_kernel(
    adj_hbm, near_hbm, far_hbm, ss_hbm, gs_hbm, pool_hbm, send_hbm, up_hbm, down_hbm,
    adj, near_ref, far_ref, ss_ref, gs_ref, pool_ref, send_ref, up_ref, down_ref, in_sems, pool_sems, out_sems,
):
    species = adj.shape[0]
    rows, elements = pool_ref.shape[1:]
    half = send_ref.shape[3] // 2
    pairs = [(near_hbm, near_ref), (ss_hbm, ss_ref)]
    pairs += [(adj_hbm.at[:, a:b, :], adj.at[:, a:b, :]) for a, b in (LOW, HIGH, MID)]
    pairs += [(far_hbm, far_ref), (gs_hbm, gs_ref)]
    copies = [pltpu.make_async_copy(x, y, in_sems.at[i]) for i, (x, y) in enumerate(pairs)]
    for copy in copies:
        copy.start()
    leaving = []

    def leave(source, target, sem):
        leaving.append(pltpu.make_async_copy(source, target, sem))
        leaving[-1].start()

    low = lax.broadcasted_iota(I32, (rows, 2 * half), 1) < half

    def exchange(q):
        a = dot(pool_ref[2 * q], one_hot(elements, ss_ref[2 * q : 2 * q + 1, :]))
        b = dot(pool_ref[2 * q + 1], one_hot(elements, ss_ref[2 * q + 1 : 2 * q + 2, :]))
        for i in range(send_ref.shape[0] // 2):
            lanes = slice(2 * half * i, 2 * half * (i + 1))
            ai, bi = a[:, lanes], b[:, lanes]
            send_ref[2 * i, q] = jnp.where(low, ai, pltpu.roll(bi, half, 1)).astype(BF16)
            send_ref[2 * i + 1, q] = jnp.where(low, pltpu.roll(ai, half, 1), bi).astype(BF16)

    def fill(faces, picks, first, last, chunk):
        count = len(faces)
        shared = species * REST
        for c in range(0, elements, chunk):
            found = [dot(picks[s], adj[s, first:last, c : c + chunk].astype(BF16)) for s in range(species)]
            rest = sum(x[MAIN * count :] for x in found)
            for i, f in enumerate(faces):
                pieces = [x[MAIN * i : MAIN * (i + 1)] for x in found] + [rest[shared * i : shared * (i + 1)]]
                pool_ref[f, :, c : c + chunk] = jnp.concatenate(pieces, axis=0).astype(BF16)

    for copy in copies[:4]:
        copy.wait()
    fill((0,), near_ref[0], *LOW, 1024)
    fill((1,), near_ref[1], *HIGH, 1024)
    exchange(0)
    leave(send_ref.at[:, 0], send_hbm.at[:, 0], out_sems.at[0])
    for f in (0, 1):
        leave(pool_ref.at[f], pool_hbm.at[f], pool_sems.at[f])
    for copy in copies[4:]:
        copy.wait()
    fill((2, 3, 4, 5), far_ref[...], 0, HIGH[1], 512)
    for f in (2, 3, 4, 5):
        leave(pool_ref.at[f], pool_hbm.at[f], pool_sems.at[f])
    down_ref[...] = dot(pool_ref[4], one_hot(elements, gs_ref[0:1, :])).astype(BF16)
    up_ref[...] = dot(pool_ref[5], one_hot(elements, gs_ref[1:2, :])).astype(BF16)
    exchange(1)
    leave(down_ref, down_hbm, out_sems.at[1])
    leave(up_ref, up_hbm, out_sems.at[2])
    leave(send_ref.at[:, 1], send_hbm.at[:, 1], out_sems.at[3])
    for copy in leaving:
        copy.wait()


def local_kernel(
    adj_ref, vel_ref, der_ref, nbr_ref, pool_hbm, tile_ref, slot_ref, base_ref, gap_ref, pool, mixed, digits, sems,
):
    step = pl.program_id(0)
    species, nodes, block = adj_ref.shape
    rows = pool.shape[1]
    group = 16
    copies = [pltpu.make_async_copy(pool_hbm.at[f], pool.at[f], sems.at[f]) for f in range(6)]

    @pl.when(step == 0)
    def _():
        for copy in copies:
            copy.start()
        for d in range(3):
            for b in range(nodes // group):
                lines = der_ref[d * nodes + b * group : d * nodes + (b + 1) * group, :]
                mixed[(3 * b + d) * group : (3 * b + d + 1) * group, :] = lines * jnp.asarray(SECTION, BF16)
        digits[...] = slot_digits(slot_ref)

    for s in range(species):
        g = dot(mixed[...], adj_ref[s].astype(BF16))
        for b in range(nodes // group):
            lines = slice(b * group, (b + 1) * group)
            total = adj_ref[s, lines]
            for d in range(3):
                total += vel_ref[d, lines].astype(F32) * g[(3 * b + d) * group : (3 * b + d + 1) * group]
            base_ref[0, s, lines] = total
    gap_ref[0, 6 * rows :] = tile_rows(tile_ref[...], digits[...])

    @pl.when(step == 0)
    def _():
        for copy in copies:
            copy.wait()

    cols = pl.ds(pl.multiple_of(step * block, block), block)
    for f in range(6):
        hot = one_hot(pool.shape[2], nbr_ref[f : f + 1, :])
        gap_ref[0, rows * f : rows * (f + 1)] = dot(pool[f ^ 1], hot) - pool[f, :, cols].astype(F32)


def slot_digits(slot_ref):
    fine = slot_ref.shape[1] // 2
    slot = jnp.transpose(slot_ref[...].astype(F32))
    upper = jnp.floor(slot * (1.0 / 64.0))
    return jnp.concatenate([
        jnp.concatenate([x[:fine], x[fine:]], axis=1) for x in (upper, slot - 64.0 * upper)
    ], axis=0).astype(BF16)


def tile_rows(tile, digits):
    fine, high = digits.shape[0] // 2, digits.shape[1] // 2
    coarse = jnp.right_shift(tile, fine.bit_length() - 1)
    place = jnp.bitwise_and(coarse, 1) * high + jnp.right_shift(coarse, 1)
    found = dot(digits, one_hot(2 * high, place))
    rows = 64.0 * found[:fine] + found[fine:]
    within = lax.broadcasted_iota(I32, rows.shape, 0) == jnp.bitwise_and(tile, fine - 1)
    return jnp.broadcast_to(jnp.sum(jnp.where(within, rows, 0.0), axis=0, keepdims=True), (8, tile.shape[1]))


def update_kernel(
    nbr_ref, gap_hbm, recv_ref, below_ref, above_ref, fs_ref, speed_ref, order_ref, lift_ref, prof_ref, base_hbm,
    next_hbm, contrib_ref, other_ref, seen_ref, rpool, lift_sorted, flux, low_next, gap_all, base_all, row_ref,
    sems, next_sems, *, elements,
):
    step = pl.program_id(0)
    peers, _, rows, width = recv_ref.shape
    half = width // 2
    steps, species, nodes, block = base_all.shape

    def loads(index):
        return (
            pltpu.make_async_copy(gap_hbm.at[index], gap_all.at[index], sems.at[0, index]),
            pltpu.make_async_copy(base_hbm.at[index], base_all.at[index], sems.at[1, index]),
        )

    def leaving(index):
        cols = pl.ds(pl.multiple_of(index * block, block), block)
        return pltpu.make_async_copy(base_all.at[index], next_hbm.at[:, :, cols], next_sems.at[index])

    def contribute(index):
        terms = [dot(prof_ref[...], low_next[s]) for s in range(species)]
        contrib = jnp.transpose(jnp.concatenate(terms, axis=0))
        high = contrib.astype(BF16)
        lines = pl.ds(index * block if isinstance(index, int) else pl.multiple_of(index * block, block), block)
        contrib_ref[lines, : contrib.shape[1]] = high
        contrib_ref[lines, contrib.shape[1] :] = (contrib - high.astype(F32)).astype(BF16)

    @pl.when(step == 0)
    def _():
        for index in range(steps):
            for copy in loads(index):
                copy.start()
        for q in range(2):
            for i in range(peers // 2):
                lanes = slice(width * i, width * (i + 1))
                x, y = recv_ref[2 * i, q], recv_ref[2 * i + 1, q]
                rpool[2 * q, :, lanes] = jnp.concatenate([x[:, :half], y[:, :half]], axis=1)
                rpool[2 * q + 1, :, lanes] = jnp.concatenate([x[:, half:], y[:, half:]], axis=1)
        lift_sorted[...] = (SECTION * jnp.transpose(dot(order_ref[...], lift_ref[...]))).astype(BF16)
        low_next[...] = jnp.zeros_like(low_next)

    for copy in loads(step):
        copy.wait()
    gap_ref, base_ref = gap_all.at[step], base_all.at[step]
    row_ref[:, pl.ds(pl.multiple_of(step * block, block), block)] = gap_ref[6 * rows : 6 * rows + 1].astype(I32)
    contribute(jnp.maximum(step - 1, 0))
    upwind = dot(speed_ref[...], jnp.maximum(fs_ref[...], jnp.zeros((), BF16)))
    slots = peers * half
    first = lax.broadcasted_iota(I32, (2 * REST, block), 0) < REST
    tails = [[] for _ in range(species)]
    for q in range(3):
        mains, rests = [], []
        for f in (2 * q, 2 * q + 1):
            t = f ^ 1
            if t < 4:
                far = dot(rpool[t], one_hot(slots, nbr_ref[f : f + 1, :] - elements))
            else:
                source = below_ref if t == 5 else above_ref
                hot = one_hot(source.shape[1], nbr_ref[f : f + 1, :] - (elements + slots))
                far = dot(source[...], hot)
            gap = gap_ref[rows * f : rows * (f + 1)] + far
            speed = upwind[MAIN * f : MAIN * (f + 1)]
            mains.append([speed * gap[MAIN * s : MAIN * (s + 1)] for s in range(species)])
            line = 6 * MAIN + species * REST * f
            rests.append(upwind[line : line + species * REST] * gap[species * MAIN :])
        for s in range(species):
            both = jnp.concatenate([mains[0][s], mains[1][s]], axis=0).astype(BF16)
            flux[s, 2 * MAIN * q : 2 * MAIN * (q + 1), :] = both
        for v in range(species // 2):
            a = rests[0][2 * REST * v : 2 * REST * (v + 1)]
            b = rests[1][2 * REST * v : 2 * REST * (v + 1)]
            tails[2 * v].append(jnp.where(first, a, pltpu.roll(b, REST, 0)))
            tails[2 * v + 1].append(jnp.where(first, pltpu.roll(a, REST, 0), b))
    for s in range(species):
        flux[s, 6 * MAIN :, :] = jnp.concatenate(tails[s], axis=0).astype(BF16)
    for s in range(species):
        value = base_ref[s] + dot(lift_sorted[...], flux[s])
        base_ref[s] = value
        low_next[s] = value.astype(BF16)
    leaving(step).start()

    @pl.when(step == steps - 1)
    def _():
        contribute(steps - 1)
        seen_ref[...] = row_ref[...]
        scatter(row_ref, contrib_ref, other_ref, True, elements - block)
        for index in range(steps):
            leaving(index).wait()


def scatter(row_ref, contrib_ref, out_ref, other, cut=0):
    width = out_ref.shape[1]
    core = lax.axis_index("core")
    side = 1 - core if other else core
    for i in range(out_ref.shape[0] // GROUP_ROWS):
        lines = row_ref[...] - (2 * i + side) * GROUP_ROWS
        both = dot(one_hot(GROUP_ROWS, lines[:, cut:]), contrib_ref[cut:])
        if cut:
            both = dot(one_hot(GROUP_ROWS, lines[:, :cut]), contrib_ref[:cut]) + both
        out_ref[i * GROUP_ROWS : (i + 1) * GROUP_ROWS, :] = both[:, :width] + both[:, width:]


def own_kernel(row_ref, contrib_ref, out_ref):
    scatter(row_ref, contrib_ref, out_ref, False)


def whole(*shape):
    return pl.BlockSpec(shape, lambda i: (0,) * len(shape))


def params(mib):
    return pltpu.CompilerParams(vmem_limit_bytes=mib * MIB)


def cost(flops, nbytes):
    return pl.CostEstimate(flops=flops, bytes_accessed=nbytes, transcendentals=0)


def on_device(
    adjoint, velocity, face_speed, derivatives, lift_operator, emission_profile,
    neighbours, sub_sends, group_sends, element_tile, tile_slot,
):
    species, nodes, elements = adjoint.shape
    peers = lax.axis_size("sub")
    groups = lax.axis_size("z") * lax.axis_size("core")
    slots = sub_sends.shape[1]
    half = slots // peers
    vcap = group_sends.shape[1]
    tiles = tile_slot.shape[0]
    heights = emission_profile.shape[1]
    face_rows = face_speed.shape[0]
    rows = species * (MAIN + REST)
    sds = jax.ShapeDtypeStruct
    block = 512
    steps = elements // block

    near = jnp.stack([trace_picker(species, (f,), *span) for f, span in enumerate((LOW, HIGH))])
    far = trace_picker(species, (2, 3, 4, 5), 0, HIGH[1])
    vmem = pl.BlockSpec(memory_space=pltpu.VMEM)
    hbm = pl.BlockSpec(memory_space=pltpu.HBM)
    made = [
        sds((6, rows, elements), BF16), sds((peers, 2, rows, 2 * half), BF16), sds((rows, vcap), BF16), sds((rows, vcap), BF16),
    ]
    pool, send, up, down = pl.pallas_call(
        send_kernel,
        in_specs=[hbm] * 5,
        out_specs=[hbm] * 4,
        out_shape=made,
        scratch_shapes=[
            pltpu.VMEM((species, HIGH[1], elements), F32),
            *(pltpu.VMEM(x.shape, x.dtype) for x in (near, far, sub_sends, group_sends, *made)),
            pltpu.SemaphoreType.DMA((7,)), pltpu.SemaphoreType.DMA((6,)), pltpu.SemaphoreType.DMA((4,)),
        ],
        compiler_params=params(60),
        cost_estimate=cost(12_000_000_000, 14_000_000),
        name="sends",
    )(
        adjoint, near, far, sub_sends, group_sends,
    )

    received = lax.all_to_all(send, "sub", split_axis=0, concat_axis=0, tiled=True)
    ring_up = [(g, (g + 1) % groups) for g in range(groups)]
    ring_down = [(g, (g - 1) % groups) for g in range(groups)]
    from_below = lax.ppermute(up, ("z", "core"), ring_up)
    from_above = lax.ppermute(down, ("z", "core"), ring_down)

    base, gap = pl.pallas_call(
        local_kernel,
        grid=(steps,),
        in_specs=[
            pl.BlockSpec((species, nodes, block), lambda i: (0, 0, i)),
            pl.BlockSpec((3, nodes, block), lambda i: (0, 0, i)),
            whole(3 * nodes, nodes),
            pl.BlockSpec((6, block), lambda i: (0, i)),
            hbm,
            pl.BlockSpec((1, block), lambda i: (0, i)), whole(tiles // 128, 128),
        ],
        out_specs=[
            pl.BlockSpec((1, species, nodes, block), lambda i: (i, 0, 0, 0)),
            pl.BlockSpec((1, 6 * rows + 8, block), lambda i: (i, 0, 0)),
        ],
        out_shape=[sds((steps, species, nodes, block), F32), sds((steps, 6 * rows + 8, block), F32)],
        scratch_shapes=[
            pltpu.VMEM((6, rows, elements), BF16), pltpu.VMEM((3 * nodes, nodes), BF16),
            pltpu.VMEM((128, 2 * tiles // 128), BF16), pltpu.SemaphoreType.DMA((6,)),
        ],
        compiler_params=params(60),
        cost_estimate=cost(16_000_000_000, 32_000_000),
        name="local",
    )(
        adjoint, velocity, derivatives, neighbours, pool, element_tile.reshape(1, elements),
        tile_slot.reshape(tiles // 128, 128),
    )

    face_nodes = face_rows // 6
    width = species * heights
    adjoint_next, contrib, for_other, seen_row = pl.pallas_call(
        functools.partial(update_kernel, elements=elements),
        grid=(steps,),
        in_specs=[
            pl.BlockSpec((6, block), lambda i: (0, i)),
            hbm, whole(peers, 2, rows, 2 * half), whole(rows, vcap), whole(rows, vcap),
            pl.BlockSpec((face_rows, block), lambda i: (0, i)),
            whole(2 * rows, face_rows), whole(face_rows, face_rows), whole(face_rows, nodes), whole(heights, nodes),
            hbm,
        ],
        out_specs=[
            hbm, whole(elements, 2 * width), whole(tiles // 2, width), whole(1, elements),
        ],
        out_shape=[
            sds((species, nodes, elements), F32), sds((elements, 2 * width), BF16), sds((tiles // 2, width), F32),
            sds((1, elements), I32),
        ],
        scratch_shapes=[
            pltpu.VMEM((4, rows, slots), BF16), pltpu.VMEM((nodes, face_rows), BF16),
            pltpu.VMEM((species, face_rows, block), BF16), pltpu.VMEM((species, nodes, block), BF16),
            pltpu.VMEM((steps, 6 * rows + 8, block), F32), pltpu.VMEM((steps, species, nodes, block), F32),
            pltpu.VMEM((1, elements), I32),
            pltpu.SemaphoreType.DMA((2, steps)), pltpu.SemaphoreType.DMA((steps,)),
        ],
        compiler_params=params(UPDATE_MIB),
        cost_estimate=cost(8_000_000_000, 28_000_000),
        name="update",
    )(
        neighbours, gap, received, from_below, from_above, face_speed, speed_picker(species, face_nodes),
        lift_picker(face_nodes), lift_operator.T, emission_profile.T, base,
    )

    theirs = lax.ppermute(for_other, "core", [(0, 1), (1, 0)])
    own = pl.pallas_call(
        own_kernel,
        in_specs=[vmem] * 2,
        out_specs=vmem,
        out_shape=sds((tiles // 2, width), F32),
        compiler_params=params(16),
        cost_estimate=cost(2_100_000_000, 2_000_000),
        name="scatter_own",
    )(seen_row, contrib)
    partial = (own + theirs).astype(BF16)
    chips = groups * peers // 2
    pieces = lax.all_to_all(
        partial.reshape(chips, tiles // 2 // chips, width), ("z", "sub"), split_axis=0, concat_axis=0
    )
    emission_grad = jnp.sum(pieces.astype(F32), axis=0)
    return adjoint_next, emission_grad


def solution(mesh):
    groups, peers = mesh.devices.shape
    mesh = Mesh(mesh.devices.reshape(groups // 2, 2, peers), ("z", "core", "sub"))
    both = ("z", "core", "sub")
    placed = (
        P(None, None, both), P(None, None, both), P(None, both), P(), P(), P(),
        P(None, both), P(None, both), P(None, both), P(both), P(),
    )
    return jax.shard_map(
        on_device,
        mesh=mesh,
        in_specs=placed,
        out_specs=(P(None, None, both), P(both, None)),
        check_vma=False,
    )
```

```python
import functools

import jax
import jax.numpy as jnp
import numpy as np
from jax import lax
from jax.experimental import pallas as pl
from jax.experimental.pallas import tpu as pltpu
from jax.sharding import Mesh, PartitionSpec as P

ORDER = 5
SECTION = 0.125
MIB = 1024 * 1024
UPDATE_MIB = 46
MAIN = 32
REST = 4
GROUP_ROWS = 512
F32, BF16, I16, I32 = jnp.float32, jnp.bfloat16, jnp.int16, jnp.int32


def face_table(order):
    edge_nodes = order + 1
    coords_a, coords_b = np.meshgrid(np.arange(edge_nodes), np.arange(edge_nodes), indexing="ij")
    coords_a = coords_a.reshape(-1)
    coords_b = coords_b.reshape(-1)
    face_rows = []
    for axis_id in range(3):
        for level_id in (0, edge_nodes - 1):
            fixed_col = coords_a * 0 + level_id
            if axis_id == 0:
                triple = (fixed_col, coords_a, coords_b)
            elif axis_id == 1:
                triple = (coords_a, fixed_col, coords_b)
            else:
                triple = (coords_a, coords_b, fixed_col)
            face_rows.append((triple[0] * edge_nodes + triple[1]) * edge_nodes + triple[2])
    return np.stack(face_rows).astype(np.int32)


def picker(columns, lines):
    out = np.zeros((len(lines), columns), np.float32)
    for row, column in enumerate(lines):
        if column is not None:
            out[row, column] = 1.0
    return jnp.asarray(out, BF16)


def trace_picker(species, faces, first, last):
    table = face_table(ORDER)
    return jnp.stack([
        picker(last - first, [table[f, k] - first for f in faces for k in range(MAIN)] + [
            table[f, MAIN + j] - first if t == s else None
            for f in faces for t in range(species) for j in range(REST)
        ])
        for s in range(species)
    ])


def speed_picker(species, face_nodes):
    lines = [f * face_nodes + k for f in range(6) for k in range(MAIN)]
    lines += [f * face_nodes + MAIN + j for f in range(6) for _ in range(species) for j in range(REST)]
    return picker(6 * face_nodes, lines)


def lift_picker(face_nodes):
    lines = [f * face_nodes + k for f in range(6) for k in range(MAIN)]
    lines += [f * face_nodes + MAIN + j for f in range(6) for j in range(REST)]
    return picker(6 * face_nodes, lines)


def one_hot(count, positions):
    rows = lax.broadcasted_iota(I16, (count, positions.shape[1]), 0)
    return jnp.where(rows == positions.astype(I16), jnp.ones((), BF16), jnp.zeros((), BF16))


def dot(a, b):
    return jnp.dot(a, b, preferred_element_type=F32)


LOW, MID, HIGH = (0, 40), (40, 176), (176, 216)


def send_kernel(
    adj_hbm, near_hbm, far_hbm, ss_hbm, gs_hbm, pool_hbm, send_hbm, mate_hbm, next_hbm,
    adj, near_ref, far_ref, ss_ref, gs_ref, pool_ref, send_ref, mate_ref, next_ref, in_sems, pool_sems, out_sems,
):
    species = adj.shape[0]
    rows, elements = pool_ref.shape[1:]
    half = send_ref.shape[3] // 2
    pairs = [(near_hbm, near_ref), (ss_hbm, ss_ref)]
    pairs += [(adj_hbm.at[:, a:b, :], adj.at[:, a:b, :]) for a, b in (LOW, HIGH, MID)]
    pairs += [(far_hbm, far_ref), (gs_hbm, gs_ref)]
    copies = [pltpu.make_async_copy(x, y, in_sems.at[i]) for i, (x, y) in enumerate(pairs)]
    for copy in copies:
        copy.start()
    leaving = []

    def leave(source, target, sem):
        leaving.append(pltpu.make_async_copy(source, target, sem))
        leaving[-1].start()

    low = lax.broadcasted_iota(I32, (rows, 2 * half), 1) < half

    def exchange(q):
        a = dot(pool_ref[2 * q], one_hot(elements, ss_ref[2 * q : 2 * q + 1, :]))
        b = dot(pool_ref[2 * q + 1], one_hot(elements, ss_ref[2 * q + 1 : 2 * q + 2, :]))
        for i in range(send_ref.shape[0] // 2):
            lanes = slice(2 * half * i, 2 * half * (i + 1))
            ai, bi = a[:, lanes], b[:, lanes]
            send_ref[2 * i, q] = jnp.where(low, ai, pltpu.roll(bi, half, 1)).astype(BF16)
            send_ref[2 * i + 1, q] = jnp.where(low, pltpu.roll(ai, half, 1), bi).astype(BF16)

    def fill(faces, picks, first, last, chunk):
        count = len(faces)
        shared = species * REST
        for c in range(0, elements, chunk):
            found = [dot(picks[s], adj[s, first:last, c : c + chunk].astype(BF16)) for s in range(species)]
            rest = sum(x[MAIN * count :] for x in found)
            for i, f in enumerate(faces):
                pieces = [x[MAIN * i : MAIN * (i + 1)] for x in found] + [rest[shared * i : shared * (i + 1)]]
                pool_ref[f, :, c : c + chunk] = jnp.concatenate(pieces, axis=0).astype(BF16)

    for copy in copies[:4]:
        copy.wait()
    fill((0,), near_ref[0], *LOW, 1024)
    fill((1,), near_ref[1], *HIGH, 1024)
    exchange(0)
    leave(send_ref.at[:, 0], send_hbm.at[:, 0], out_sems.at[0])
    for f in (0, 1):
        leave(pool_ref.at[f], pool_hbm.at[f], pool_sems.at[f])
    for copy in copies[4:]:
        copy.wait()
    fill((2, 3, 4, 5), far_ref[...], 0, HIGH[1], 512)
    for f in (2, 3, 4, 5):
        leave(pool_ref.at[f], pool_hbm.at[f], pool_sems.at[f])
    core = lax.axis_index("core")
    for target, upper in ((mate_ref, 1 - core), (next_ref, core)):
        target[...] = dot(pool_ref[4 + upper], one_hot(elements, gs_ref[pl.ds(upper, 1), :])).astype(BF16)
    exchange(1)
    leave(mate_ref, mate_hbm, out_sems.at[1])
    leave(next_ref, next_hbm, out_sems.at[2])
    leave(send_ref.at[:, 1], send_hbm.at[:, 1], out_sems.at[3])
    for copy in leaving:
        copy.wait()


def local_kernel(
    adj_ref, vel_ref, der_ref, nbr_ref, pool_hbm, tile_ref, slot_ref, base_ref, gap_ref, pool, mixed, digits, sems,
):
    step = pl.program_id(0)
    species, nodes, block = adj_ref.shape
    rows = pool.shape[1]
    group = 16
    copies = [pltpu.make_async_copy(pool_hbm.at[f], pool.at[f], sems.at[f]) for f in range(6)]

    @pl.when(step == 0)
    def _():
        for copy in copies:
            copy.start()
        for d in range(3):
            for b in range(nodes // group):
                lines = der_ref[d * nodes + b * group : d * nodes + (b + 1) * group, :]
                mixed[(3 * b + d) * group : (3 * b + d + 1) * group, :] = lines * jnp.asarray(SECTION, BF16)
        digits[...] = slot_digits(slot_ref)

    for s in range(species):
        g = dot(mixed[...], adj_ref[s].astype(BF16))
        for b in range(nodes // group):
            lines = slice(b * group, (b + 1) * group)
            total = adj_ref[s, lines]
            for d in range(3):
                total += vel_ref[d, lines].astype(F32) * g[(3 * b + d) * group : (3 * b + d + 1) * group]
            base_ref[0, s, lines] = total
    gap_ref[0, 6 * rows :] = tile_rows(tile_ref[...], digits[...])

    @pl.when(step == 0)
    def _():
        for copy in copies:
            copy.wait()

    cols = pl.ds(pl.multiple_of(step * block, block), block)
    for f in range(6):
        hot = one_hot(pool.shape[2], nbr_ref[f : f + 1, :])
        gap_ref[0, rows * f : rows * (f + 1)] = dot(pool[f ^ 1], hot) - pool[f, :, cols].astype(F32)


def slot_digits(slot_ref):
    fine = slot_ref.shape[1] // 2
    slot = jnp.transpose(slot_ref[...].astype(F32))
    upper = jnp.floor(slot * (1.0 / 64.0))
    return jnp.concatenate([
        jnp.concatenate([x[:fine], x[fine:]], axis=1) for x in (upper, slot - 64.0 * upper)
    ], axis=0).astype(BF16)


def tile_rows(tile, digits):
    fine, high = digits.shape[0] // 2, digits.shape[1] // 2
    coarse = jnp.right_shift(tile, fine.bit_length() - 1)
    place = jnp.bitwise_and(coarse, 1) * high + jnp.right_shift(coarse, 1)
    found = dot(digits, one_hot(2 * high, place))
    rows = 64.0 * found[:fine] + found[fine:]
    within = lax.broadcasted_iota(I32, rows.shape, 0) == jnp.bitwise_and(tile, fine - 1)
    return jnp.broadcast_to(jnp.sum(jnp.where(within, rows, 0.0), axis=0, keepdims=True), (8, tile.shape[1]))


def update_kernel(
    nbr_ref, gap_hbm, recv_ref, mate_ref, near_ref, fs_ref, speed_ref, order_ref, lift_ref, prof_ref, base_hbm,
    next_hbm, contrib_ref, other_ref, seen_ref, rpool, lift_sorted, flux, low_next, gap_all, base_all, row_ref,
    sems, next_sems, *, elements,
):
    step = pl.program_id(0)
    peers, _, rows, width = recv_ref.shape
    half = width // 2
    steps, species, nodes, block = base_all.shape

    def loads(index):
        return (
            pltpu.make_async_copy(gap_hbm.at[index], gap_all.at[index], sems.at[0, index]),
            pltpu.make_async_copy(base_hbm.at[index], base_all.at[index], sems.at[1, index]),
        )

    def leaving(index):
        cols = pl.ds(pl.multiple_of(index * block, block), block)
        return pltpu.make_async_copy(base_all.at[index], next_hbm.at[:, :, cols], next_sems.at[index])

    def contribute(index):
        terms = [dot(prof_ref[...], low_next[s]) for s in range(species)]
        contrib = jnp.transpose(jnp.concatenate(terms, axis=0))
        high = contrib.astype(BF16)
        lines = pl.ds(index * block if isinstance(index, int) else pl.multiple_of(index * block, block), block)
        contrib_ref[lines, : contrib.shape[1]] = high
        contrib_ref[lines, contrib.shape[1] :] = (contrib - high.astype(F32)).astype(BF16)

    @pl.when(step == 0)
    def _():
        for index in range(steps):
            for copy in loads(index):
                copy.start()
        for q in range(2):
            for i in range(peers // 2):
                lanes = slice(width * i, width * (i + 1))
                x, y = recv_ref[2 * i, q], recv_ref[2 * i + 1, q]
                rpool[2 * q, :, lanes] = jnp.concatenate([x[:, :half], y[:, :half]], axis=1)
                rpool[2 * q + 1, :, lanes] = jnp.concatenate([x[:, half:], y[:, half:]], axis=1)
        lift_sorted[...] = (SECTION * jnp.transpose(dot(order_ref[...], lift_ref[...]))).astype(BF16)
        low_next[...] = jnp.zeros_like(low_next)

    for copy in loads(step):
        copy.wait()
    gap_ref, base_ref = gap_all.at[step], base_all.at[step]
    row_ref[:, pl.ds(pl.multiple_of(step * block, block), block)] = gap_ref[6 * rows : 6 * rows + 1].astype(I32)
    contribute(jnp.maximum(step - 1, 0))
    upwind = dot(speed_ref[...], jnp.maximum(fs_ref[...], jnp.zeros((), BF16)))
    slots = peers * half
    core = lax.axis_index("core")
    first = lax.broadcasted_iota(I32, (2 * REST, block), 0) < REST
    tails = [[] for _ in range(species)]
    for q in range(3):
        mains, rests = [], []
        for f in (2 * q, 2 * q + 1):
            t = f ^ 1
            if t < 4:
                far = dot(rpool[t], one_hot(slots, nbr_ref[f : f + 1, :] - elements))
            else:
                mine = core == (1 if t == 5 else 0)
                source = jnp.where(mine, mate_ref[...].astype(F32), near_ref[...].astype(F32)).astype(BF16)
                hot = one_hot(source.shape[1], nbr_ref[f : f + 1, :] - (elements + slots))
                far = dot(source, hot)
            gap = gap_ref[rows * f : rows * (f + 1)] + far
            speed = upwind[MAIN * f : MAIN * (f + 1)]
            mains.append([speed * gap[MAIN * s : MAIN * (s + 1)] for s in range(species)])
            line = 6 * MAIN + species * REST * f
            rests.append(upwind[line : line + species * REST] * gap[species * MAIN :])
        for s in range(species):
            both = jnp.concatenate([mains[0][s], mains[1][s]], axis=0).astype(BF16)
            flux[s, 2 * MAIN * q : 2 * MAIN * (q + 1), :] = both
        for v in range(species // 2):
            a = rests[0][2 * REST * v : 2 * REST * (v + 1)]
            b = rests[1][2 * REST * v : 2 * REST * (v + 1)]
            tails[2 * v].append(jnp.where(first, a, pltpu.roll(b, REST, 0)))
            tails[2 * v + 1].append(jnp.where(first, pltpu.roll(a, REST, 0), b))
    for s in range(species):
        flux[s, 6 * MAIN :, :] = jnp.concatenate(tails[s], axis=0).astype(BF16)
    for s in range(species):
        value = base_ref[s] + dot(lift_sorted[...], flux[s])
        base_ref[s] = value
        low_next[s] = value.astype(BF16)
    leaving(step).start()

    @pl.when(step == steps - 1)
    def _():
        contribute(steps - 1)
        seen_ref[...] = row_ref[...]
        scatter(row_ref, contrib_ref, other_ref, True, elements - block)
        for index in range(steps):
            leaving(index).wait()


def scatter(row_ref, contrib_ref, out_ref, other, cut=0):
    width = out_ref.shape[1]
    core = lax.axis_index("core")
    side = 1 - core if other else core
    for i in range(out_ref.shape[0] // GROUP_ROWS):
        lines = row_ref[...] - (2 * i + side) * GROUP_ROWS
        both = dot(one_hot(GROUP_ROWS, lines[:, cut:]), contrib_ref[cut:])
        if cut:
            both = dot(one_hot(GROUP_ROWS, lines[:, :cut]), contrib_ref[:cut]) + both
        out_ref[i * GROUP_ROWS : (i + 1) * GROUP_ROWS, :] = both[:, :width] + both[:, width:]


def own_kernel(row_ref, contrib_ref, out_ref):
    scatter(row_ref, contrib_ref, out_ref, False)


def whole(*shape):
    return pl.BlockSpec(shape, lambda i: (0,) * len(shape))


def params(mib):
    return pltpu.CompilerParams(vmem_limit_bytes=mib * MIB)


def cost(flops, nbytes):
    return pl.CostEstimate(flops=flops, bytes_accessed=nbytes, transcendentals=0)


def on_device(
    adjoint, velocity, face_speed, derivatives, lift_operator, emission_profile,
    neighbours, sub_sends, group_sends, element_tile, tile_slot,
):
    species, nodes, elements = adjoint.shape
    peers = lax.axis_size("sub")
    groups = lax.axis_size("z") * lax.axis_size("core")
    slots = sub_sends.shape[1]
    half = slots // peers
    vcap = group_sends.shape[1]
    tiles = tile_slot.shape[0]
    heights = emission_profile.shape[1]
    face_rows = face_speed.shape[0]
    rows = species * (MAIN + REST)
    sds = jax.ShapeDtypeStruct
    block = 512
    steps = elements // block

    near = jnp.stack([trace_picker(species, (f,), *span) for f, span in enumerate((LOW, HIGH))])
    far = trace_picker(species, (2, 3, 4, 5), 0, HIGH[1])
    vmem = pl.BlockSpec(memory_space=pltpu.VMEM)
    hbm = pl.BlockSpec(memory_space=pltpu.HBM)
    made = [
        sds((6, rows, elements), BF16), sds((peers, 2, rows, 2 * half), BF16), sds((rows, vcap), BF16), sds((rows, vcap), BF16),
    ]
    pool, send, for_mate, for_next = pl.pallas_call(
        send_kernel,
        in_specs=[hbm] * 5,
        out_specs=[hbm] * 4,
        out_shape=made,
        scratch_shapes=[
            pltpu.VMEM((species, HIGH[1], elements), F32),
            *(pltpu.VMEM(x.shape, x.dtype) for x in (near, far, sub_sends, group_sends, *made)),
            pltpu.SemaphoreType.DMA((7,)), pltpu.SemaphoreType.DMA((6,)), pltpu.SemaphoreType.DMA((4,)),
        ],
        compiler_params=params(60),
        cost_estimate=cost(12_000_000_000, 14_000_000),
        name="sends",
    )(
        adjoint, near, far, sub_sends, group_sends,
    )

    received = lax.all_to_all(send, "sub", split_axis=0, concat_axis=0, tiled=True)
    across = [(g, (g + 1 if g % 2 else g - 1) % groups) for g in range(groups)]
    from_mate = lax.ppermute(for_mate, "core", [(0, 1), (1, 0)])
    from_next = lax.ppermute(for_next, ("z", "core"), across)

    base, gap = pl.pallas_call(
        local_kernel,
        grid=(steps,),
        in_specs=[
            pl.BlockSpec((species, nodes, block), lambda i: (0, 0, i)),
            pl.BlockSpec((3, nodes, block), lambda i: (0, 0, i)),
            whole(3 * nodes, nodes),
            pl.BlockSpec((6, block), lambda i: (0, i)),
            hbm,
            pl.BlockSpec((1, block), lambda i: (0, i)), whole(tiles // 128, 128),
        ],
        out_specs=[
            pl.BlockSpec((1, species, nodes, block), lambda i: (i, 0, 0, 0)),
            pl.BlockSpec((1, 6 * rows + 8, block), lambda i: (i, 0, 0)),
        ],
        out_shape=[sds((steps, species, nodes, block), F32), sds((steps, 6 * rows + 8, block), F32)],
        scratch_shapes=[
            pltpu.VMEM((6, rows, elements), BF16), pltpu.VMEM((3 * nodes, nodes), BF16),
            pltpu.VMEM((128, 2 * tiles // 128), BF16), pltpu.SemaphoreType.DMA((6,)),
        ],
        compiler_params=params(60),
        cost_estimate=cost(16_000_000_000, 32_000_000),
        name="local",
    )(
        adjoint, velocity, derivatives, neighbours, pool, element_tile.reshape(1, elements),
        tile_slot.reshape(tiles // 128, 128),
    )

    face_nodes = face_rows // 6
    width = species * heights
    adjoint_next, contrib, for_other, seen_row = pl.pallas_call(
        functools.partial(update_kernel, elements=elements),
        grid=(steps,),
        in_specs=[
            pl.BlockSpec((6, block), lambda i: (0, i)),
            hbm, whole(peers, 2, rows, 2 * half), whole(rows, vcap), whole(rows, vcap),
            pl.BlockSpec((face_rows, block), lambda i: (0, i)),
            whole(2 * rows, face_rows), whole(face_rows, face_rows), whole(face_rows, nodes), whole(heights, nodes),
            hbm,
        ],
        out_specs=[
            hbm, whole(elements, 2 * width), whole(tiles // 2, width), whole(1, elements),
        ],
        out_shape=[
            sds((species, nodes, elements), F32), sds((elements, 2 * width), BF16), sds((tiles // 2, width), F32),
            sds((1, elements), I32),
        ],
        scratch_shapes=[
            pltpu.VMEM((4, rows, slots), BF16), pltpu.VMEM((nodes, face_rows), BF16),
            pltpu.VMEM((species, face_rows, block), BF16), pltpu.VMEM((species, nodes, block), BF16),
            pltpu.VMEM((steps, 6 * rows + 8, block), F32), pltpu.VMEM((steps, species, nodes, block), F32),
            pltpu.VMEM((1, elements), I32),
            pltpu.SemaphoreType.DMA((2, steps)), pltpu.SemaphoreType.DMA((steps,)),
        ],
        compiler_params=params(UPDATE_MIB),
        cost_estimate=cost(8_000_000_000, 28_000_000),
        name="update",
    )(
        neighbours, gap, received, from_mate, from_next, face_speed, speed_picker(species, face_nodes),
        lift_picker(face_nodes), lift_operator.T, emission_profile.T, base,
    )

    theirs = lax.ppermute(for_other, "core", [(0, 1), (1, 0)])
    own = pl.pallas_call(
        own_kernel,
        in_specs=[vmem] * 2,
        out_specs=vmem,
        out_shape=sds((tiles // 2, width), F32),
        compiler_params=params(16),
        cost_estimate=cost(2_100_000_000, 2_000_000),
        name="scatter_own",
    )(seen_row, contrib)
    partial = (own + theirs).astype(BF16)
    chips = groups * peers // 2
    pieces = lax.all_to_all(
        partial.reshape(chips, tiles // 2 // chips, width), ("z", "sub"), split_axis=0, concat_axis=0
    )
    emission_grad = jnp.sum(pieces.astype(F32), axis=0)
    return adjoint_next, emission_grad


def solution(mesh):
    groups, peers = mesh.devices.shape
    mesh = Mesh(mesh.devices.reshape(groups // 2, 2, peers), ("z", "core", "sub"))
    both = ("z", "core", "sub")
    placed = (
        P(None, None, both), P(None, None, both), P(None, both), P(), P(), P(),
        P(None, both), P(None, both), P(None, both), P(both), P(),
    )
    return jax.shard_map(
        on_device,
        mesh=mesh,
        in_specs=placed,
        out_specs=(P(None, None, both), P(both, None)),
        check_vma=False,
    )
```
